256 devices in a mesh: row: 8 (over y, x_lo), col: 32 (over x_hi, z, core).
Axes of the slice: x: 4 (x_hi: 2, x_lo: 2; x = x_hi * 2 + x_lo), y: 4, z: 8, core: 2. Of those that a mesh axis runs over, the one named last changes fastest.
Arguments:
- inv_sep: bfloat16 [24576, 24576], P('row', 'col'), may hold values from -6 to 6
- lower_one: bfloat16 [24576, 256], P('col', 'row'), may hold values from -0.0390625 to 0.0390625
- upper_one: bfloat16 [256, 24576], P('col', 'row'), may hold values from -0.0390625 to 0.0390625
- diag_inv_one: float32 [256, 256], replicated, may hold values from -6 to 6
- blocks_one: int32 [160], replicated, may hold values from 0 to 191, as said below
- lower_two: bfloat16 [24576, 256], P('col', 'row'), may hold values from -0.046875 to 0.046875
- upper_two: bfloat16 [256, 24576], P('col', 'row'), may hold values from -0.046875 to 0.046875
- corner_lower: bfloat16 [256, 256], replicated, may hold values from -0.375 to 0.375
- corner_upper: bfloat16 [256, 256], replicated, may hold values from -0.375 to 0.375
- diag_inv_two: float32 [256, 256], replicated, may hold values from -6 to 6
- blocks_two: int32 [128], replicated, may hold values from 0 to 191, as said below
Outputs:
- inv_lower_one: bfloat16 [20480, 256], P(('row', 'col'))
- inv_upper_one: bfloat16 [256, 20480], P('row', 'col')
- inv_diag_one: float32 [256, 256], replicated
- inv_lower_two: bfloat16 [16384, 256], P(('row', 'col'))
- inv_upper_two: bfloat16 [256, 16384], P('row', 'col')
- inv_diag_two: float32 [256, 256], replicated
The draws below stay inside these ranges and needn't reach their ends.
Inputs may be any that keep to these rules, and one draw needn't show every extreme that they name: `blocks_one`: distinct block indices in increasing order; each aligned run of 6 blocks holds exactly 5 of them; the first and the last block of the separator are listed. `blocks_two`: distinct block indices in increasing order, each of them also in blocks_one; each aligned run of 6 blocks holds exactly 4 of them; the first and the last block of the separator are listed.
All inputs are finite; a program needn't handle non-finite values.
Results may differ from the reference program's by a relative error of at most 0.0039.
Values may be sent and summed in bfloat16 or wider, within the bound.
A program may use at most 64 MiB of HBM per device.

```python
import jax
import jax.numpy as jnp
from jax import lax

NS = 24576
W = 256
B = 128
SPAN = 6
PICK_ONE = 5
PICK_TWO = 4
LIST_ONE = 160
LIST_TWO = 128


def block_lists(key):
    run_count = NS // B // SPAN
    run_keys = jax.random.split(key, 2 * run_count)

    def one_run(run_id, head_key, tail_key):
        random_head = jax.random.randint(head_key, (), 0, SPAN)
        head_block = jnp.where(run_id == 0, 0, jnp.where(run_id == run_count - 1, SPAN - 1, random_head)).astype(jnp.int32)
        tail_blocks = jax.random.permutation(tail_key, SPAN - 1).astype(jnp.int32)
        tail_blocks = tail_blocks + (tail_blocks >= head_block).astype(jnp.int32)
        ordering = jnp.concatenate([head_block[None], tail_blocks])
        listed_one = run_id * SPAN + jnp.sort(ordering[:PICK_ONE])
        listed_two = run_id * SPAN + jnp.sort(ordering[:PICK_TWO])
        return (listed_one, listed_two)
    listed_one, listed_two = jax.vmap(one_run)(jnp.arange(run_count, dtype=jnp.int32), run_keys[:run_count], run_keys[run_count:])
    return (listed_one.reshape(-1).astype(jnp.int32), listed_two.reshape(-1).astype(jnp.int32))


def draw_blocks_one(key, part):
    return block_lists(jax.random.fold_in(key, 11))[0]


def draw_blocks_two(key, part):
    return block_lists(jax.random.fold_in(key, 11))[1]


def with_spikes(array, rng, source, target, shards_of, factor):
    owner, partner = [(jnp.arange(array.shape[dim]) // (array.shape[dim] // shards_of)).reshape([-1 if axis == dim else 1 for axis in range(array.ndim)]) for dim in (source, target)]
    chosen = jax.random.permutation(rng, shards_of)[partner]
    strong = (owner == chosen) | (owner == (partner + shards_of // 2) % shards_of)
    return jnp.where(strong, factor * array, array)


def levels(key, dims, cuts, smallest, high):
    factor_of, own = 1.0, jax.random.fold_in(key, 6)
    for position, shards_of in cuts:
        heights = jnp.exp(jax.random.uniform(jax.random.fold_in(own, position), (shards_of,), jnp.float32, smallest / len(cuts), high / len(cuts)))
        factor_of = factor_of * jnp.repeat(heights, dims[position] // shards_of).reshape([-1 if axis == position else 1 for axis in range(len(dims))])
    return factor_of


def scatter_about(own_key, shape, width, reach, cuts=(), kind=jnp.bfloat16):
    drawn = width * jax.random.normal(own_key, shape, jnp.float32)
    if cuts:
        drawn = drawn * levels(own_key, shape, cuts, -0.22, 0.18)
    return jnp.clip(drawn, -reach, reach).astype(kind)


def heavy_noise(stream_key, extent, deviation, reach, cuts, heavy, held_as=jnp.bfloat16):
    array = deviation * jax.random.normal(stream_key, extent, jnp.float32)
    if cuts:
        array = array * levels(stream_key, extent, cuts, -0.22, 0.18)
    return jnp.clip(with_spikes(array, jax.random.fold_in(stream_key, 3), *heavy), -reach, reach).astype(held_as)


def setup_inputs(seed: int = 0) -> dict:
    seeds = jax.random.split(jax.random.key(seed), 12)
    inv_sep = heavy_noise(seeds[0], (NS, NS), 1.0, 6.0, ((0, 8), (1, 32)), (1, 0, 32, 2.75))
    lower_one = scatter_about(seeds[1], (NS, W), (LIST_ONE * B) ** -0.5, 0.0390625, ((0, 32), (1, 8)))
    upper_one = scatter_about(seeds[2], (W, NS), (LIST_ONE * B) ** -0.5, 0.0390625, ((0, 32), (1, 8)))
    diag_inv_one = scatter_about(seeds[3], (W, W), 1.0, 6.0, (), jnp.float32)
    blocks_one = draw_blocks_one(jax.random.fold_in(seeds[11], 71), 0)
    lower_two = scatter_about(seeds[5], (NS, W), (LIST_TWO * B) ** -0.5, 0.046875, ((0, 32), (1, 8)))
    upper_two = scatter_about(seeds[6], (W, NS), (LIST_TWO * B) ** -0.5, 0.046875, ((0, 32), (1, 8)))
    corner_lower = scatter_about(seeds[7], (W, W), W ** -0.5, 0.375)
    corner_upper = scatter_about(seeds[8], (W, W), W ** -0.5, 0.375)
    diag_inv_two = scatter_about(seeds[9], (W, W), 1.0, 6.0, (), jnp.float32)
    blocks_two = draw_blocks_two(jax.random.fold_in(seeds[11], 71), 0)
    return {"inv_sep": inv_sep, "lower_one": lower_one, "upper_one": upper_one, "diag_inv_one": diag_inv_one, "blocks_one": blocks_one, "lower_two": lower_two, "upper_two": upper_two, "corner_lower": corner_lower, "corner_upper": corner_upper, "diag_inv_two": diag_inv_two, "blocks_two": blocks_two}


def block_rows(blocks):
    return (blocks[:, None] * B + jnp.arange(B, dtype=jnp.int32)[None, :]).reshape(-1).astype(jnp.int32)


def highest(first_mat, second_mat):
    return jnp.dot(first_mat.astype(jnp.float32), second_mat.astype(jnp.float32), precision=lax.Precision.HIGHEST)


def rows_times(inv_sep, blocks, panel_mat):
    columns = block_rows(blocks)

    def one_block(block_id):
        row_block = lax.dynamic_slice_in_dim(inv_sep, (block_id * B).astype(jnp.int32), B, 0)
        return highest(jnp.take(row_block, columns, axis=1), panel_mat)

    return lax.map(one_block, blocks).reshape(blocks.shape[0] * B, panel_mat.shape[1])


def left_times(panel_mat, inv_sep, blocks):
    columns = block_rows(blocks)
    pieces = jnp.transpose(panel_mat.reshape(panel_mat.shape[0], blocks.shape[0], B), (1, 0, 2))

    def add_block(summed, paired):
        row_block = lax.dynamic_slice_in_dim(inv_sep, (paired[0] * B).astype(jnp.int32), B, 0)
        return summed + highest(paired[1], jnp.take(row_block, columns, axis=1)), None

    summed, _ = lax.scan(add_block, jnp.zeros((panel_mat.shape[0], columns.shape[0]), jnp.float32), (blocks, pieces))
    return summed


def reference(inv_sep, lower_one, upper_one, diag_inv_one, blocks_one, lower_two, upper_two, corner_lower, corner_upper, diag_inv_two, blocks_two):
    rows_one = block_rows(blocks_one)
    rows_two = block_rows(blocks_two)
    places = jnp.sum((blocks_one[None, :] < blocks_two[:, None]).astype(jnp.int32), axis=1).astype(jnp.int32)
    positions = block_rows(places)
    lower_p = jnp.take(lower_one, rows_one, axis=0)
    upper_p = jnp.take(upper_one, rows_one, axis=1)
    lower_c = jnp.take(lower_two, rows_two, axis=0)
    upper_c = jnp.take(upper_two, rows_two, axis=1)
    inv_lower_one = (-rows_times(inv_sep, blocks_one, lower_p)).astype(jnp.bfloat16)
    inv_upper_one = (-left_times(upper_p, inv_sep, blocks_one)).astype(jnp.bfloat16)
    inv_diag_one = diag_inv_one - highest(upper_p, inv_lower_one)
    ancestor_rows = jnp.take(inv_lower_one, positions, axis=0)
    ancestor_cols = jnp.take(inv_upper_one, positions, axis=1)
    inv_lower_two = (-(rows_times(inv_sep, blocks_two, lower_c) + highest(ancestor_rows, corner_lower))).astype(jnp.bfloat16)
    inv_upper_two = (-(left_times(upper_c, inv_sep, blocks_two) + highest(corner_upper, ancestor_cols))).astype(jnp.bfloat16)
    corner_inv = -(highest(ancestor_cols, lower_c) + highest(inv_diag_one, corner_lower))
    inv_diag_two = diag_inv_two - (highest(upper_c, inv_lower_two) + highest(corner_upper, corner_inv))
    return inv_lower_one, inv_upper_one, inv_diag_one, inv_lower_two, inv_upper_two, inv_diag_two
```

```python
import functools

import jax
import jax.numpy as jnp
from jax import lax
from jax.experimental import pallas as pl
from jax.experimental.pallas import tpu as pltpu
from jax.sharding import PartitionSpec as P

B = 128
SPAN = 6
ONE = 5
TWO = 4
XH = 2
CORES = 2
MESH = pl.DeviceIdType.MESH
F32 = jnp.float32
BF16 = jnp.bfloat16


def mm(a, b):
    return jnp.dot(a, b, preferred_element_type=F32)


def exact(a, b):
    return jnp.dot(
        a, b, preferred_element_type=F32, precision=lax.Precision.HIGHEST
    )


def kernel(
    R,
    C,
    W,
    sel_any,
    sel2_any,
    own_u,
    own_x,
    pick_cols,
    cl_ref,
    cu_ref,
    dg1_ref,
    dg2_ref,
    l1_out,
    u1_out,
    d1_out,
    l2_out,
    u2_out,
    d2_out,
    sel,
    sel2,
    G,
    V,
    XG,
    X,
    Pm,
    cr,
    xs,
    xr,
    zs,
    zr,
    own,
    PU,
    PUb,
    ur_buf,
    dd,
    drc,
    dxs,
    drx,
    dz,
    Dall,
    tail,
    sem_sel,
    gz_s,
    gz_r,
    gx_s,
    gx_r,
    gc_s,
    gc_r,
    xg_s,
    xg_r,
    cs_s,
    cs_r,
    rx_s,
    rx_r,
    rz_s,
    rz_r,
    pu_s,
    pu_r,
    d_s,
    d_r,
    dz_s,
    dz_r,
    dr_s,
    dr_r,
):
    Z = C // (XH * CORES)
    runs = C // R
    nb1, nb2 = runs * ONE, runs * TWO
    ncol = ONE * B
    ur = W // C
    lw = W // R
    s1, s2 = ONE * B // R, TWO * B // R
    M = XH * Z
    uw = W // R

    r = lax.axis_index("row")
    c = lax.axis_index("col")
    k = lax.rem(c, CORES)
    z = lax.rem(c // CORES, Z)
    xh = c // (CORES * Z)

    def col_of(xh_, z_, k_):
        return (xh_ * Z + z_) * CORES + k_

    core_dev = (r, col_of(xh, z, 1 - k))
    x_dev = (r, col_of(1 - xh, z, k))

    def z_at(i):
        return lax.rem(z + 1 + i, Z)

    def r_at(i):
        return lax.rem(r + 1 + i, R)

    def z_dev(zz):
        return (r, col_of(xh, zz, k))

    def row_dev(rr):
        return (rr, c)

    def rcopy(src, dst, ssem, rsem, dev):
        return pltpu.make_async_remote_copy(
            src_ref=src,
            dst_ref=dst,
            send_sem=ssem,
            recv_sem=rsem,
            device_id=dev,
            device_id_type=MESH,
        )

    def loop(n, body):
        def step(i, carry):
            body(i)
            return carry

        lax.fori_loop(0, n, step, 0)

    sel_copy = pltpu.make_async_copy(sel_any, sel, sem_sel.at[0])
    sel2_copy = pltpu.make_async_copy(sel2_any, sel2, sem_sel.at[1])
    sel_copy.start()
    sel2_copy.start()

    barrier = pltpu.get_barrier_semaphore()
    pl.semaphore_signal(barrier, inc=1, device_id=core_dev, device_id_type=MESH)
    pl.semaphore_signal(barrier, inc=1, device_id=x_dev, device_id_type=MESH)

    def greet_z(i):
        pl.semaphore_signal(barrier, inc=1, device_id=z_dev(z_at(i)), device_id_type=MESH)

    def greet_r(i):
        pl.semaphore_signal(barrier, inc=1, device_id=row_dev(r_at(i)), device_id_type=MESH)

    loop(Z - 1, greet_z)
    loop(R - 1, greet_r)

    for half in range(2):
        G[half, c] = own_u[half]
        XG[half, r] = own_x[half]

    pl.semaphore_wait(barrier, 2 + (Z - 1) + (R - 1))

    def gz(src_z, to_z):
        slot = col_of(xh, src_z, k)
        return rcopy(G.at[:, slot], G.at[:, slot], gz_s.at[to_z], gz_r.at[src_z], z_dev(to_z))

    def gx(src_xh, src_z):
        slot = col_of(src_xh, src_z, k)
        return rcopy(G.at[:, slot], G.at[:, slot], gx_s.at[src_z], gx_r.at[src_z], x_dev)

    def gc(src_xh, src_z, src_k):
        slot = col_of(src_xh, src_z, src_k)
        sem = src_xh * Z + src_z
        return rcopy(G.at[:, slot], G.at[:, slot], gc_s.at[sem], gc_r.at[sem], core_dev)

    def xg(src_r, to_r):
        return rcopy(
            XG.at[:, src_r], XG.at[:, src_r], xg_s.at[to_r], xg_r.at[src_r], row_dev(to_r)
        )

    loop(R - 1, lambda i: xg(r, r_at(i)).start())
    loop(Z - 1, lambda i: gz(z, z_at(i)).start())
    gx(xh, z).start()
    gc(xh, z, k).start()

    loop(R - 1, lambda i: xg(r_at(i), r).wait_recv())
    x1t = XG[0].reshape(W, ncol)
    lct = XG[1].reshape(W, ncol)
    clt = cl_ref[...].astype(F32).T.astype(BF16)
    x2 = (lct.astype(F32) - mm(clt, x1t)).T
    x2hi = x2.astype(BF16)
    X[:, 0:W] = x1t.astype(F32).T.astype(BF16)
    X[:, W : 2 * W] = x2hi
    X[:, 2 * W : 3 * W] = (x2 - x2hi.astype(F32)).astype(BF16)

    def cs(m):
        return rcopy(Pm.at[m, 1 - k], cr.at[m], cs_s.at[m], cs_r.at[m], core_dev)

    sel_copy.wait()
    sel2_copy.wait()

    def lower(m):
        first = sel[pl.ds(pl.multiple_of(m * (2 * s1), 16), 2 * s1), :]
        p1 = mm(first, X[:, 0:W])
        Pm[m, 0, 0:s1, :] = p1[0:s1]
        Pm[m, 1, 0:s1, :] = p1[s1:]
        rows = sel2[pl.ds(pl.multiple_of(m * (2 * s2), 16), 2 * s2), :]
        p2 = mm(rows, X[:, W : 2 * W]) + mm(rows, X[:, 2 * W : 3 * W])
        Pm[m, 0, s1 : s1 + s2, :] = p2[0:s2]
        Pm[m, 1, s1 : s1 + s2, :] = p2[s2:]
        cs(m).start()

    loop(Z, lambda i: lower((1 - xh) * Z + z_at(i)))

    def pass_on(i):
        lower(xh * Z + z_at(i))

        @pl.when(i < Z - 1)
        def _():
            zz = z_at(i)
            gz(zz, z).wait_recv()
            gx(xh, zz).start()
            gc(xh, zz, k).start()

    loop(Z, pass_on)

    def rx(zz):
        return rcopy(xs.at[zz], xr.at[zz], rx_s.at[zz], rx_r.at[zz], x_dev)

    def rz(src_z, to_z):
        return rcopy(zs.at[to_z], zr.at[src_z], rz_s.at[to_z], rz_r.at[src_z], z_dev(to_z))

    def to_x(i):
        zz = z_at(i)
        m = (1 - xh) * Z + zz
        cs(m).wait_recv()
        xs[zz] = (Pm[m, k] + cr[m]).astype(BF16)
        rx(zz).start()

    loop(Z, to_x)

    def to_z(i):
        zz = z_at(i)
        m = xh * Z + zz
        cs(m).wait_recv()
        rx(zz).wait_recv()
        total = Pm[m, k] + cr[m] + xr[zz].astype(F32)

        @pl.when(i < Z - 1)
        def _():
            zs[zz] = total.astype(BF16)
            rz(z, zz).start()

        @pl.when(i == Z - 1)
        def _():
            own[...] = total

        zg = lax.rem(z + i, Z)
        gx(1 - xh, zg).wait_recv()
        gc(1 - xh, zg, k).start()

    loop(Z, to_z)

    def all_in(i):
        gc(i // Z, lax.rem(i, Z), 1 - k).wait_recv()

    loop(M, all_in)
    cu = cu_ref[...]
    wide = 2 * B if nb1 % 2 == 0 else B

    def second(j):
        at = pl.ds(pl.multiple_of(j * wide, wide), wide)
        up = G[0, :, :, at].reshape(W, wide)
        uc = G[1, :, :, at].reshape(W, wide)
        v = uc.astype(F32) - mm(cu, up)
        hi = v.astype(BF16)
        V[0, :, at] = up
        V[1, :, at] = hi
        V[2, :, at] = (v - hi.astype(F32)).astype(BF16)

    loop(nb1 * B // wide, second)

    def upper(j):
        PU[j] = mm(V[j], sel[...])

    loop(3, upper)
    PU[1] = PU[1] + PU[2]
    PUb[0] = PU[0].astype(BF16).reshape(R, uw, ncol)
    PUb[1] = PU[1].astype(BF16).reshape(R, uw, ncol)

    def pu(src_r, to_r):
        return rcopy(PUb.at[:, to_r], ur_buf.at[:, src_r], pu_s.at[to_r], pu_r.at[src_r], row_dev(to_r))

    loop(R - 1, lambda i: pu(r, r_at(i)).start())

    tail[...] = dg2_ref[...] + exact(
        cu.astype(F32), exact(dg1_ref[...], cl_ref[...].astype(F32))
    )

    def from_z(i):
        zz = z_at(i)
        rz(zz, z).wait_recv()
        own[...] = own[...] + zr[zz].astype(F32)

    loop(Z - 1, from_z)
    l1_out[...] = (-own[0:s1, :]).astype(BF16)
    l2_out[...] = (-own[s1 : s1 + s2, :]).astype(BF16)

    mine = pl.ds(pl.multiple_of(r * uw, 16), uw)

    def from_r(i):
        rr = r_at(i)
        pu(rr, r).wait_recv()
        PU[0, mine, :] = PU[0, mine, :] + ur_buf[0, rr].astype(F32)
        PU[1, mine, :] = PU[1, mine, :] + ur_buf[1, rr].astype(F32)

    loop(R - 1, from_r)
    u1 = (-PU[0, mine, :]).astype(BF16)
    u2 = (-PU[1, mine, :]).astype(BF16)
    dd[0] = mm(u1, X[:, 0:W])
    dd[1] = mm(u2, X[:, W : 2 * W]) + mm(u2, X[:, 2 * W : 3 * W])
    d_core = rcopy(dd.at[1 - k], drc, d_s.at[0], d_r.at[0], core_dev)
    d_core.start()
    u1_out[...] = u1
    u2_out[...] = mm(u2, pick_cols[...]).astype(BF16)

    d_core.wait_recv()
    dxs[...] = dd[k] + drc[...]
    d_x = rcopy(dxs, drx, d_s.at[1], d_r.at[1], x_dev)
    d_x.start()
    d_x.wait_recv()
    dz[z] = dxs[...] + drx[...]

    def dzc(src_z, to_z):
        return rcopy(dz.at[src_z], dz.at[src_z], dz_s.at[to_z], dz_r.at[src_z], z_dev(to_z))

    loop(Z - 1, lambda i: dzc(z, z_at(i)).start())
    loop(Z - 1, lambda i: dzc(z_at(i), z).wait_recv())
    total = dz[0]
    for i in range(1, Z):
        total = total + dz[i]
    Dall[k, r] = total

    def drow(src_r, to_r):
        return rcopy(
            Dall.at[k, src_r], Dall.at[k, src_r], dr_s.at[to_r], dr_r.at[src_r], row_dev(to_r)
        )

    loop(R - 1, lambda i: drow(r, r_at(i)).start())
    loop(R - 1, lambda i: drow(r_at(i), r).wait_recv())

    def d_both(src_k):
        return rcopy(Dall.at[src_k], Dall.at[src_k], d_s.at[2], d_r.at[2], core_dev)

    d_both(k).start()
    d_both(1 - k).wait_recv()
    d1_out[...] = dg1_ref[...] - Dall[0].reshape(W, W)
    d2_out[...] = tail[...] - Dall[1].reshape(W, W)

    def left_z(i):
        zz = z_at(i)
        gz(z, zz).wait_send()
        rz(z, zz).wait_send()
        dzc(z, zz).wait_send()

    def left_r(i):
        rr = r_at(i)
        xg(r, rr).wait_send()
        pu(r, rr).wait_send()
        drow(r, rr).wait_send()

    def left_x(i):
        gx(xh, i).wait_send()
        rx(i).wait_send()

    def left_c(i):
        gc(i // Z, lax.rem(i, Z), k).wait_send()
        cs(i).wait_send()

    loop(Z - 1, left_z)
    loop(R - 1, left_r)
    loop(Z, left_x)
    loop(M, left_c)
    d_core.wait_send()
    d_x.wait_send()
    d_both(k).wait_send()


def pick(
    R,
    C,
    one_ref,
    two_ref,
    sep,
    lp_ref,
    lc_ref,
    up_ref,
    uc_ref,
    sel,
    sel2,
    own_u,
    own_x,
    pick_cols,
):
    r = lax.axis_index("row")
    c = lax.axis_index("col")
    runs = C // R
    nb1 = runs * ONE
    ur = up_ref.shape[0]
    lw = lp_ref.shape[0]

    def one_at(run, s):
        return one_ref[run * ONE + s]

    def two_at(run, t):
        return two_ref[run * TWO + t]

    def in_two(run, b):
        hit = (two_at(run, 0) == b).astype(jnp.int32)
        for t in range(1, TWO):
            hit = hit + (two_at(run, t) == b).astype(jnp.int32)
        return hit

    col_at = [pl.multiple_of((one_at(c, s) - c * SPAN) * B, B) for s in range(ONE)]

    def row_at(b):
        return pl.multiple_of((b - r * (runs * SPAN)) * B, B)

    def some_run(q, carry):
        run = r * runs + q
        for s in range(ONE):
            b = one_at(run, s)
            at = row_at(b)
            to = pl.ds(pl.multiple_of((q * ONE + s) * B, B), B)
            for t in range(ONE):
                sel[to, t * B : (t + 1) * B] = sep[pl.ds(at, B), pl.ds(col_at[t], B)]
            own_u[0, :, to] = up_ref[:, pl.ds(at, B)]
            piece = uc_ref[:, pl.ds(at, B)].astype(F32)
            hit = jnp.full((ur, B), in_two(run, b))
            own_u[1, :, to] = jnp.where(hit > 0, piece, 0.0).astype(BF16)
        for t in range(TWO):
            at = row_at(two_at(run, t))
            to = pl.ds(pl.multiple_of((q * TWO + t) * B, B), B)
            for s in range(ONE):
                sel2[to, s * B : (s + 1) * B] = sep[pl.ds(at, B), pl.ds(col_at[s], B)]
        return carry

    lax.fori_loop(0, runs, some_run, 0)

    same = lax.broadcasted_iota(jnp.int32, (B, B), 0) == lax.broadcasted_iota(jnp.int32, (B, B), 1)
    eye = jnp.where(same, 1.0, 0.0)
    for s in range(ONE):
        b = one_at(c, s)
        to = pl.ds(s * B, B)
        own_x[0, :, to] = lp_ref[:, pl.ds(col_at[s], B)]
        piece = lc_ref[:, pl.ds(col_at[s], B)].astype(F32)
        hit = jnp.full((lw, B), in_two(c, b))
        own_x[1, :, to] = jnp.where(hit > 0, piece, 0.0).astype(BF16)
        for t in range(TWO):
            hit = jnp.full((B, B), (two_at(c, t) == b).astype(jnp.int32))
            pick_cols[to, t * B : (t + 1) * B] = jnp.where(hit > 0, eye, 0.0).astype(BF16)


def on_device(
    R,
    C,
    inv_sep,
    lower_one,
    upper_one,
    diag_inv_one,
    blocks_one,
    lower_two,
    upper_two,
    corner_lower,
    corner_upper,
    diag_inv_two,
    blocks_two,
):
    W = diag_inv_one.shape[0]
    Z = C // (XH * CORES)
    M = XH * Z
    runs = C // R
    nb1 = runs * ONE
    ncol = ONE * B
    ur, lw, uw = W // C, W // R, W // R
    s1, s2 = ONE * B // R, TWO * B // R
    sh = s1 + s2
    vmem = pl.BlockSpec(memory_space=pltpu.VMEM)
    smem = pl.BlockSpec(memory_space=pltpu.SMEM)
    dma = pltpu.SemaphoreType.DMA
    picked = pl.pallas_call(
        functools.partial(pick, R, C),
        out_shape=(
            jax.ShapeDtypeStruct((nb1 * B, ncol), BF16),
            jax.ShapeDtypeStruct((runs * TWO * B, ncol), BF16),
            jax.ShapeDtypeStruct((2, ur, nb1 * B), BF16),
            jax.ShapeDtypeStruct((2, lw, ncol), BF16),
            jax.ShapeDtypeStruct((ncol, TWO * B), BF16),
        ),
        in_specs=[smem, smem] + [vmem] * 5,
        out_specs=(vmem,) * 5,
        compiler_params=pltpu.CompilerParams(vmem_limit_bytes=24 * 2**20),
        name="pick",
    )(blocks_one, blocks_two, inv_sep, lower_one.T, lower_two.T, upper_one, upper_two)
    return pl.pallas_call(
        functools.partial(kernel, R, C, W),
        out_shape=(
            jax.ShapeDtypeStruct((s1, W), BF16),
            jax.ShapeDtypeStruct((uw, ncol), BF16),
            jax.ShapeDtypeStruct((W, W), F32),
            jax.ShapeDtypeStruct((s2, W), BF16),
            jax.ShapeDtypeStruct((uw, TWO * B), BF16),
            jax.ShapeDtypeStruct((W, W), F32),
        ),
        in_specs=[pl.BlockSpec(memory_space=pl.ANY)] * 2 + [vmem] * 7,
        out_specs=(vmem,) * 6,
        scratch_shapes=[
            pltpu.VMEM((nb1 * B, ncol), BF16),
            pltpu.VMEM((runs * TWO * B, ncol), BF16),
            pltpu.VMEM((2, C, ur, nb1 * B), BF16),
            pltpu.VMEM((3, W, nb1 * B), BF16),
            pltpu.VMEM((2, R, lw, ncol), BF16),
            pltpu.VMEM((ncol, 3 * W), BF16),
            pltpu.VMEM((M, 2, sh, W), F32),
            pltpu.VMEM((M, sh, W), F32),
            pltpu.VMEM((Z, sh, W), BF16),
            pltpu.VMEM((Z, sh, W), BF16),
            pltpu.VMEM((Z, sh, W), BF16),
            pltpu.VMEM((Z, sh, W), BF16),
            pltpu.VMEM((sh, W), F32),
            pltpu.VMEM((3, W, ncol), F32),
            pltpu.VMEM((2, R, uw, ncol), BF16),
            pltpu.VMEM((2, R, uw, ncol), BF16),
            pltpu.VMEM((2, uw, W), F32),
            pltpu.VMEM((uw, W), F32),
            pltpu.VMEM((uw, W), F32),
            pltpu.VMEM((uw, W), F32),
            pltpu.VMEM((Z, uw, W), F32),
            pltpu.VMEM((2, R, uw, W), F32),
            pltpu.VMEM((W, W), F32),
        ]
        + [dma((n,)) for n in (2, Z, Z, Z, Z, M, M, R, R, M, M, Z, Z, Z, Z, R, R, 3, 3, Z, Z, R, R)],
        compiler_params=pltpu.CompilerParams(
            collective_id=0, has_side_effects=True, vmem_limit_bytes=40 * 2**20
        ),
        name="panels",
    )(*picked, corner_lower, corner_upper, diag_inv_one, diag_inv_two)


def solution(mesh):
    R, C = mesh.shape["row"], mesh.shape["col"]
    return jax.shard_map(
        functools.partial(on_device, R, C),
        mesh=mesh,
        in_specs=(
            P("row", "col"),
            P("col", "row"),
            P("col", "row"),
            P(),
            P(),
            P("col", "row"),
            P("col", "row"),
            P(),
            P(),
            P(),
            P(),
        ),
        out_specs=(
            P(("row", "col"), None),
            P("row", "col"),
            P(),
            P(("row", "col"), None),
            P("row", "col"),
            P(),
        ),
        check_vma=False,
    )
```

```python
import functools

import jax
import jax.numpy as jnp
from jax import lax
from jax.experimental import pallas as pl
from jax.experimental.pallas import tpu as pltpu
from jax.sharding import PartitionSpec as P

B = 128
SPAN = 6
ONE = 5
TWO = 4
XH = 2
CORES = 2
XL = 2
MESH = pl.DeviceIdType.MESH
F32 = jnp.float32
BF16 = jnp.bfloat16


def mm(a, b):
    return jnp.dot(a, b, preferred_element_type=F32)


def exact(a, b):
    return jnp.dot(
        a, b, preferred_element_type=F32, precision=lax.Precision.HIGHEST
    )


def kernel(
    R,
    C,
    W,
    sel_any,
    sel2_any,
    own_u,
    own_x,
    pick_cols,
    cl_ref,
    cu_ref,
    dg1_ref,
    dg2_ref,
    l1_out,
    u1_out,
    d1_out,
    l2_out,
    u2_out,
    d2_out,
    sel,
    sel2,
    G,
    V,
    XG,
    X,
    Pm,
    cr,
    xs,
    xr,
    zs,
    zr,
    own,
    PU,
    PUb,
    ur_buf,
    dd,
    drc,
    dxs,
    drx,
    dz,
    Dall,
    tail,
    sem_sel,
    xs_s,
    xs_r,
    xy_s,
    xy_r,
    ap_s,
    am_s,
    a_r,
    bp_s,
    bm_s,
    b_r,
    ax_s,
    ax_r,
    ac_s,
    ac_r,
    bc_s,
    bc_r,
    bx_s,
    bx_r,
    cs_s,
    cs_r,
    rx_s,
    rx_r,
    rz_s,
    rz_r,
    pu_s,
    pu_r,
    d_s,
    d_r,
    dz_s,
    dz_r,
    dr_s,
    dr_r,
):
    Z = C // (XH * CORES)
    runs = C // R
    nb1, nb2 = runs * ONE, runs * TWO
    ncol = ONE * B
    ur = W // C
    lw = W // R
    s1, s2 = ONE * B // R, TWO * B // R
    M = XH * Z
    uw = W // R

    r = lax.axis_index("row")
    c = lax.axis_index("col")
    k = lax.rem(c, CORES)
    z = lax.rem(c // CORES, Z)
    xh = c // (CORES * Z)
    Y = R // XL
    y = r // XL
    xl = lax.rem(r, XL)

    def col_of(xh_, z_, k_):
        return (xh_ * Z + z_) * CORES + k_

    core_dev = (r, col_of(xh, z, 1 - k))
    x_dev = (r, col_of(1 - xh, z, k))

    def z_at(i):
        return lax.rem(z + 1 + i, Z)

    def r_at(i):
        return lax.rem(r + 1 + i, R)

    def z_dev(zz):
        return (r, col_of(xh, zz, k))

    def row_dev(rr):
        return (rr, c)

    def rcopy(src, dst, ssem, rsem, dev):
        return pltpu.make_async_remote_copy(
            src_ref=src,
            dst_ref=dst,
            send_sem=ssem,
            recv_sem=rsem,
            device_id=dev,
            device_id_type=MESH,
        )

    def loop(n, body):
        def step(i, carry):
            body(i)
            return carry

        lax.fori_loop(0, n, step, 0)

    sel_copy = pltpu.make_async_copy(sel_any, sel, sem_sel.at[0])
    sel2_copy = pltpu.make_async_copy(sel2_any, sel2, sem_sel.at[1])
    sel_copy.start()
    sel2_copy.start()

    barrier = pltpu.get_barrier_semaphore()
    pl.semaphore_signal(barrier, inc=1, device_id=core_dev, device_id_type=MESH)
    pl.semaphore_signal(barrier, inc=1, device_id=x_dev, device_id_type=MESH)

    def greet_z(i):
        pl.semaphore_signal(barrier, inc=1, device_id=z_dev(z_at(i)), device_id_type=MESH)

    def greet_r(i):
        pl.semaphore_signal(barrier, inc=1, device_id=row_dev(r_at(i)), device_id_type=MESH)

    loop(Z - 1, greet_z)
    loop(R - 1, greet_r)

    for half in range(2):
        G[half, xh, z, k] = own_u[half]
        XG[half, y, xl] = own_x[half]

    pl.semaphore_wait(barrier, 2 + (Z - 1) + (R - 1))

    near = (y * XL + 1 - xl, c)

    def xgx(src_xl):
        return rcopy(XG.at[:, y, src_xl], XG.at[:, y, src_xl], xs_s.at[0], xs_r.at[0], near)

    def y_at(i):
        return lax.rem(y + 1 + i, Y)

    def xgy(src_y, to_y):
        return rcopy(
            XG.at[:, src_y], XG.at[:, src_y], xy_s.at[to_y], xy_r.at[src_y], (to_y * XL + xl, c)
        )

    far_p, far_m = Z // 2, Z // 2 - 1
    z_next = lax.rem(z + 1, Z)
    z_prev = lax.rem(z + Z - 1, Z)

    def behind(t):
        return lax.rem(z + Z - 1 - t, Z)

    def ahead(t):
        return lax.rem(z + 1 + t, Z)

    def a_ring(src_z, sems, to):
        block = G.at[0, xh, src_z, k]
        return rcopy(block, block, sems.at[src_z], a_r.at[src_z], z_dev(to))

    def b_ring(src_z, sems, to):
        block = G.at[1, :, src_z, k]
        return rcopy(block, block, sems.at[src_z], b_r.at[src_z], z_dev(to))

    def a_x(src_xh, src_z):
        block = G.at[0, src_xh, src_z, k]
        return rcopy(block, block, ax_s.at[src_z], ax_r.at[src_z], x_dev)

    def a_core(src_xh, src_z, src_k):
        block = G.at[0, src_xh, src_z, src_k]
        n = src_xh * Z + src_z
        return rcopy(block, block, ac_s.at[n], ac_r.at[n], core_dev)

    def b_core(src_z, src_k):
        block = G.at[1, :, src_z, src_k]
        return rcopy(block, block, bc_s.at[src_z], bc_r.at[src_z], core_dev)

    def b_x(src_xh):
        block = G.at[1, src_xh, z, k]
        return rcopy(block, block, bx_s.at[0], bx_r.at[0], x_dev)

    b_x(xh).start()
    xgx(xl).start()
    a_ring(z, ap_s, z_next).start()
    if far_m > 0:
        a_ring(z, am_s, z_prev).start()
    a_x(xh, z).start()
    a_core(xh, z, k).start()
    xgx(1 - xl).wait_recv()
    loop(Y - 1, lambda i: xgy(y, y_at(i)).start())
    b_x(1 - xh).wait_recv()
    b_ring(z, bp_s, z_next).start()
    if far_m > 0:
        b_ring(z, bm_s, z_prev).start()
    b_core(z, k).start()
    for t in range(far_p):
        zz = behind(t)
        a_ring(zz, ap_s, z_next).wait_recv()
        if t < far_p - 1:
            a_ring(zz, ap_s, z_next).start()
        a_x(xh, zz).start()
        a_core(xh, zz, k).start()
        if t < far_m:
            zz = ahead(t)
            a_ring(zz, am_s, z_prev).wait_recv()
            if t < far_m - 1:
                a_ring(zz, am_s, z_prev).start()
            a_x(xh, zz).start()
            a_core(xh, zz, k).start()
        zz = behind(t)
        b_ring(zz, bp_s, z_next).wait_recv()
        if t < far_p - 1:
            b_ring(zz, bp_s, z_next).start()
        b_core(zz, k).start()
        if t < far_m:
            zz = ahead(t)
            b_ring(zz, bm_s, z_prev).wait_recv()
            if t < far_m - 1:
                b_ring(zz, bm_s, z_prev).start()
            b_core(zz, k).start()

    loop(Y - 1, lambda i: xgy(y_at(i), y).wait_recv())
    x1t = XG[0].reshape(W, ncol)
    lct = XG[1].reshape(W, ncol)
    clt = cl_ref[...].astype(F32).T.astype(BF16)
    x2 = (lct.astype(F32) - mm(clt, x1t)).T
    x2hi = x2.astype(BF16)
    X[:, 0:W] = x1t.astype(F32).T.astype(BF16)
    X[:, W : 2 * W] = x2hi
    X[:, 2 * W : 3 * W] = (x2 - x2hi.astype(F32)).astype(BF16)

    def cs(m):
        return rcopy(Pm.at[m, 1 - k], cr.at[m], cs_s.at[m], cs_r.at[m], core_dev)

    sel_copy.wait()
    sel2_copy.wait()

    def lower(m):
        first = sel[pl.ds(pl.multiple_of(m * (2 * s1), 16), 4 * s1), :]
        p1 = mm(first, X[:, 0:W])
        rows = sel2[pl.ds(pl.multiple_of(m * (2 * s2), 16), 4 * s2), :]
        p2 = mm(rows, X[:, W : 2 * W]) + mm(rows, X[:, 2 * W : 3 * W])
        for j in range(2):
            for core in range(CORES):
                n = 2 * j + core
                Pm[m + j, core, 0:s1, :] = p1[n * s1 : (n + 1) * s1]
                Pm[m + j, core, s1 : s1 + s2, :] = p2[n * s2 : (n + 1) * s2]
            cs(m + j).start()

    def pair_at(i):
        return 2 * lax.rem(z // 2 + 1 + i, Z // 2)

    loop(Z // 2, lambda i: lower((1 - xh) * Z + pair_at(i)))
    loop(Z // 2, lambda i: lower(xh * Z + pair_at(i)))

    def rx(zz):
        return rcopy(xs.at[zz], xr.at[zz], rx_s.at[zz], rx_r.at[zz], x_dev)

    def rz(src_z, to_z):
        return rcopy(zs.at[to_z], zr.at[src_z], rz_s.at[to_z], rz_r.at[src_z], z_dev(to_z))

    def to_x(i):
        zz = z_at(i)
        m = (1 - xh) * Z + zz
        cs(m).wait_recv()
        xs[zz] = (Pm[m, k] + cr[m]).astype(BF16)
        rx(zz).start()

    loop(Z, to_x)

    def over(i):
        zz = z_at(i)
        a_x(1 - xh, zz).wait_recv()
        a_core(1 - xh, zz, k).start()

    loop(Z, over)
    loop(Z, lambda i: b_core(i, 1 - k).wait_recv())
    loop(M, lambda i: a_core(i // Z, lax.rem(i, Z), 1 - k).wait_recv())
    cu = cu_ref[...]
    wide = 2 * B if nb1 % 2 == 0 else B

    def second(j):
        at = pl.ds(pl.multiple_of(j * wide, wide), wide)
        up = G[0, :, :, :, :, at].reshape(W, wide)
        uc = G[1, :, :, :, :, at].reshape(W, wide)
        v = uc.astype(F32) - mm(cu, up)
        hi = v.astype(BF16)
        V[0, :, at] = up
        V[1, :, at] = hi
        V[2, :, at] = (v - hi.astype(F32)).astype(BF16)

    loop(nb1 * B // wide, second)

    def upper(j):
        PU[j] = mm(V[j], sel[...])

    loop(3, upper)
    PU[1] = PU[1] + PU[2]
    PUb[0] = PU[0].astype(BF16).reshape(R, uw, ncol)
    PUb[1] = PU[1].astype(BF16).reshape(R, uw, ncol)

    def pu(src_r, to_r):
        return rcopy(PUb.at[:, to_r], ur_buf.at[:, src_r], pu_s.at[to_r], pu_r.at[src_r], row_dev(to_r))

    loop(R - 1, lambda i: pu(r, r_at(i)).start())

    def to_z(i):
        zz = z_at(i)
        m = xh * Z + zz
        cs(m).wait_recv()
        rx(zz).wait_recv()
        total = Pm[m, k] + cr[m] + xr[zz].astype(F32)

        @pl.when(i < Z - 1)
        def _():
            zs[zz] = total.astype(BF16)
            rz(z, zz).start()

        @pl.when(i == Z - 1)
        def _():
            own[...] = total

    loop(Z, to_z)


    tail[...] = dg2_ref[...] + exact(
        cu.astype(F32), exact(dg1_ref[...], cl_ref[...].astype(F32))
    )

    mine = pl.ds(pl.multiple_of(r * uw, 16), uw)

    def from_r(i):
        rr = r_at(i)
        pu(rr, r).wait_recv()
        PU[0, mine, :] = PU[0, mine, :] + ur_buf[0, rr].astype(F32)
        PU[1, mine, :] = PU[1, mine, :] + ur_buf[1, rr].astype(F32)

    loop(R - 1, from_r)
    u1 = (-PU[0, mine, :]).astype(BF16)
    u2 = (-PU[1, mine, :]).astype(BF16)
    dd[0] = mm(u1, X[:, 0:W])
    dd[1] = mm(u2, X[:, W : 2 * W]) + mm(u2, X[:, 2 * W : 3 * W])
    d_core = rcopy(dd.at[1 - k], drc, d_s.at[0], d_r.at[0], core_dev)
    d_core.start()
    u1_out[...] = u1
    u2_out[...] = mm(u2, pick_cols[...]).astype(BF16)

    d_core.wait_recv()
    dxs[...] = dd[k] + drc[...]
    d_x = rcopy(dxs, drx, d_s.at[1], d_r.at[1], x_dev)
    d_x.start()
    d_x.wait_recv()
    dz[z] = (dxs[...] + drx[...]).astype(BF16)

    def dzc(src_z, to_z):
        return rcopy(dz.at[src_z], dz.at[src_z], dz_s.at[to_z], dz_r.at[src_z], z_dev(to_z))

    loop(Z - 1, lambda i: dzc(z, z_at(i)).start())
    loop(Z - 1, lambda i: dzc(z_at(i), z).wait_recv())
    total = dz[0].astype(F32)
    for i in range(1, Z):
        total = total + dz[i].astype(F32)
    Dall[k, r] = total

    def drow(src_r, to_r):
        return rcopy(
            Dall.at[k, src_r], Dall.at[k, src_r], dr_s.at[to_r], dr_r.at[src_r], row_dev(to_r)
        )

    loop(R - 1, lambda i: drow(r, r_at(i)).start())
    def from_z(i):
        zz = z_at(i)
        rz(zz, z).wait_recv()
        own[...] = own[...] + zr[zz].astype(F32)

    loop(Z - 1, from_z)
    l1_out[...] = (-own[0:s1, :]).astype(BF16)
    l2_out[...] = (-own[s1 : s1 + s2, :]).astype(BF16)

    loop(R - 1, lambda i: drow(r_at(i), r).wait_recv())

    def d_both(src_k):
        return rcopy(Dall.at[src_k], Dall.at[src_k], d_s.at[2], d_r.at[2], core_dev)

    d_both(k).start()
    d_both(1 - k).wait_recv()
    d1_out[...] = dg1_ref[...] - Dall[0].reshape(W, W)
    d2_out[...] = tail[...] - Dall[1].reshape(W, W)

    def left_z(i):
        zz = z_at(i)
        rz(z, zz).wait_send()
        dzc(z, zz).wait_send()

    def left_r(i):
        rr = r_at(i)
        pu(r, rr).wait_send()
        drow(r, rr).wait_send()

    def left_x(i):
        a_x(xh, i).wait_send()
        rx(i).wait_send()
        b_core(i, k).wait_send()

    def left_c(i):
        a_core(i // Z, lax.rem(i, Z), k).wait_send()
        cs(i).wait_send()

    b_x(xh).wait_send()
    xgx(xl).wait_send()
    loop(Y - 1, lambda i: xgy(y, y_at(i)).wait_send())
    for t in range(far_p):
        a_ring(lax.rem(z + Z - t, Z), ap_s, z_next).wait_send()
        b_ring(lax.rem(z + Z - t, Z), bp_s, z_next).wait_send()
    for t in range(far_m):
        a_ring(lax.rem(z + t, Z), am_s, z_prev).wait_send()
        b_ring(lax.rem(z + t, Z), bm_s, z_prev).wait_send()
    loop(Z - 1, left_z)
    loop(R - 1, left_r)
    loop(Z, left_x)
    loop(M, left_c)
    d_core.wait_send()
    d_x.wait_send()
    d_both(k).wait_send()


def pick(
    R,
    C,
    one_ref,
    two_ref,
    sep,
    lp_ref,
    lc_ref,
    up_ref,
    uc_ref,
    sel,
    sel2,
    own_u,
    own_x,
    pick_cols,
):
    r = lax.axis_index("row")
    c = lax.axis_index("col")
    runs = C // R
    nb1 = runs * ONE
    ur = up_ref.shape[0]
    lw = lp_ref.shape[0]

    def one_at(run, s):
        return one_ref[run * ONE + s]

    def two_at(run, t):
        return two_ref[run * TWO + t]

    def in_two(run, b):
        hit = (two_at(run, 0) == b).astype(jnp.int32)
        for t in range(1, TWO):
            hit = hit + (two_at(run, t) == b).astype(jnp.int32)
        return hit

    col_at = [pl.multiple_of((one_at(c, s) - c * SPAN) * B, B) for s in range(ONE)]

    def row_at(b):
        return pl.multiple_of((b - r * (runs * SPAN)) * B, B)

    def some_run(q, carry):
        run = r * runs + q
        for s in range(ONE):
            b = one_at(run, s)
            at = row_at(b)
            to = pl.ds(pl.multiple_of((q * ONE + s) * B, B), B)
            for t in range(ONE):
                sel[to, t * B : (t + 1) * B] = sep[pl.ds(at, B), pl.ds(col_at[t], B)]
            own_u[0, :, to] = up_ref[:, pl.ds(at, B)]
            piece = uc_ref[:, pl.ds(at, B)].astype(F32)
            hit = jnp.full((ur, B), in_two(run, b))
            own_u[1, :, to] = jnp.where(hit > 0, piece, 0.0).astype(BF16)
        for t in range(TWO):
            at = row_at(two_at(run, t))
            to = pl.ds(pl.multiple_of((q * TWO + t) * B, B), B)
            for s in range(ONE):
                sel2[to, s * B : (s + 1) * B] = sep[pl.ds(at, B), pl.ds(col_at[s], B)]
        return carry

    lax.fori_loop(0, runs, some_run, 0)

    same = lax.broadcasted_iota(jnp.int32, (B, B), 0) == lax.broadcasted_iota(jnp.int32, (B, B), 1)
    eye = jnp.where(same, 1.0, 0.0)
    for s in range(ONE):
        b = one_at(c, s)
        to = pl.ds(s * B, B)
        own_x[0, :, to] = lp_ref[:, pl.ds(col_at[s], B)]
        piece = lc_ref[:, pl.ds(col_at[s], B)].astype(F32)
        hit = jnp.full((lw, B), in_two(c, b))
        own_x[1, :, to] = jnp.where(hit > 0, piece, 0.0).astype(BF16)
        for t in range(TWO):
            hit = jnp.full((B, B), (two_at(c, t) == b).astype(jnp.int32))
            pick_cols[to, t * B : (t + 1) * B] = jnp.where(hit > 0, eye, 0.0).astype(BF16)


def on_device(
    R,
    C,
    inv_sep,
    lower_one,
    upper_one,
    diag_inv_one,
    blocks_one,
    lower_two,
    upper_two,
    corner_lower,
    corner_upper,
    diag_inv_two,
    blocks_two,
):
    W = diag_inv_one.shape[0]
    Z = C // (XH * CORES)
    M = XH * Z
    runs = C // R
    nb1 = runs * ONE
    ncol = ONE * B
    ur, lw, uw = W // C, W // R, W // R
    s1, s2 = ONE * B // R, TWO * B // R
    sh = s1 + s2
    vmem = pl.BlockSpec(memory_space=pltpu.VMEM)
    smem = pl.BlockSpec(memory_space=pltpu.SMEM)
    dma = pltpu.SemaphoreType.DMA
    picked = pl.pallas_call(
        functools.partial(pick, R, C),
        out_shape=(
            jax.ShapeDtypeStruct((nb1 * B, ncol), BF16),
            jax.ShapeDtypeStruct((runs * TWO * B, ncol), BF16),
            jax.ShapeDtypeStruct((2, ur, nb1 * B), BF16),
            jax.ShapeDtypeStruct((2, lw, ncol), BF16),
            jax.ShapeDtypeStruct((ncol, TWO * B), BF16),
        ),
        in_specs=[smem, smem] + [vmem] * 5,
        out_specs=(vmem,) * 5,
        compiler_params=pltpu.CompilerParams(vmem_limit_bytes=24 * 2**20),
        name="pick",
    )(blocks_one, blocks_two, inv_sep, lower_one.T, lower_two.T, upper_one, upper_two)
    return pl.pallas_call(
        functools.partial(kernel, R, C, W),
        out_shape=(
            jax.ShapeDtypeStruct((s1, W), BF16),
            jax.ShapeDtypeStruct((uw, ncol), BF16),
            jax.ShapeDtypeStruct((W, W), F32),
            jax.ShapeDtypeStruct((s2, W), BF16),
            jax.ShapeDtypeStruct((uw, TWO * B), BF16),
            jax.ShapeDtypeStruct((W, W), F32),
        ),
        in_specs=[pl.BlockSpec(memory_space=pl.ANY)] * 2 + [vmem] * 7,
        out_specs=(vmem,) * 6,
        scratch_shapes=[
            pltpu.VMEM((nb1 * B, ncol), BF16),
            pltpu.VMEM((runs * TWO * B, ncol), BF16),
            pltpu.VMEM((2, XH, Z, CORES, ur, nb1 * B), BF16),
            pltpu.VMEM((3, W, nb1 * B), BF16),
            pltpu.VMEM((2, R // XL, XL, lw, ncol), BF16),
            pltpu.VMEM((ncol, 3 * W), BF16),
            pltpu.VMEM((M, 2, sh, W), F32),
            pltpu.VMEM((M, sh, W), F32),
            pltpu.VMEM((Z, sh, W), BF16),
            pltpu.VMEM((Z, sh, W), BF16),
            pltpu.VMEM((Z, sh, W), BF16),
            pltpu.VMEM((Z, sh, W), BF16),
            pltpu.VMEM((sh, W), F32),
            pltpu.VMEM((3, W, ncol), F32),
            pltpu.VMEM((2, R, uw, ncol), BF16),
            pltpu.VMEM((2, R, uw, ncol), BF16),
            pltpu.VMEM((2, uw, W), F32),
            pltpu.VMEM((uw, W), F32),
            pltpu.VMEM((uw, W), F32),
            pltpu.VMEM((uw, W), F32),
            pltpu.VMEM((Z, uw, W), BF16),
            pltpu.VMEM((2, R, uw, W), F32),
            pltpu.VMEM((W, W), F32),
        ]
        + [dma((n,)) for n in (2, 1, 1, R // XL, R // XL)]
        + [dma((n,)) for n in (Z, Z, Z, Z, Z, Z, Z, Z, M, M, Z, Z, 1, 1)]
        + [dma((n,)) for n in (M, M, Z, Z, Z, Z, R, R, 3, 3, Z, Z, R, R)],
        compiler_params=pltpu.CompilerParams(
            collective_id=0, has_side_effects=True, vmem_limit_bytes=40 * 2**20
        ),
        name="panels",
    )(*picked, corner_lower, corner_upper, diag_inv_one, diag_inv_two)


def solution(mesh):
    R, C = mesh.shape["row"], mesh.shape["col"]
    return jax.shard_map(
        functools.partial(on_device, R, C),
        mesh=mesh,
        in_specs=(
            P("row", "col"),
            P("col", "row"),
            P("col", "row"),
            P(),
            P(),
            P("col", "row"),
            P("col", "row"),
            P(),
            P(),
            P(),
            P(),
        ),
        out_specs=(
            P(("row", "col"), None),
            P("row", "col"),
            P(),
            P(("row", "col"), None),
            P("row", "col"),
            P(),
        ),
        check_vma=False,
    )
```

```python
import functools

import jax
import jax.numpy as jnp
from jax import lax
from jax.experimental import pallas as pl
from jax.experimental.pallas import tpu as pltpu
from jax.sharding import PartitionSpec as P

B = 128
SPAN = 6
ONE = 5
TWO = 4
XH = 2
CORES = 2
XL = 2
MESH = pl.DeviceIdType.MESH
F32 = jnp.float32
BF16 = jnp.bfloat16


def mm(a, b):
    return jnp.dot(a, b, preferred_element_type=F32)


def exact(a, b):
    return jnp.dot(
        a, b, preferred_element_type=F32, precision=lax.Precision.HIGHEST
    )


def kernel(
    R,
    C,
    W,
    sel_any,
    sel2_any,
    own_u,
    own_x,
    pick_cols,
    cl_ref,
    cu_ref,
    dg1_ref,
    dg2_ref,
    l1_out,
    u1_out,
    d1_out,
    l2_out,
    u2_out,
    d2_out,
    sel,
    sel2,
    G,
    V,
    XG,
    X,
    Pm,
    cr,
    xs,
    xr,
    zs,
    zr,
    own,
    PU,
    PUb,
    ur_buf,
    dd,
    drc,
    dz,
    Dall,
    tail,
    sem_sel,
    xs_s,
    xs_r,
    xy_s,
    xy_r,
    ap_s,
    am_s,
    a_r,
    bp_s,
    bm_s,
    b_r,
    ax_s,
    ax_r,
    ac_s,
    ac_r,
    bc_s,
    bc_r,
    bx_s,
    bx_r,
    cs_s,
    cs_r,
    rx_s,
    rx_r,
    rz_s,
    rz_r,
    pu_s,
    pu_r,
    d_s,
    d_r,
    dz_s,
    dz_r,
    dr_s,
    dr_r,
    df_s,
    df_r,
):
    Z = C // (XH * CORES)
    runs = C // R
    nb1, nb2 = runs * ONE, runs * TWO
    ncol = ONE * B
    ur = W // C
    lw = W // R
    s1, s2 = ONE * B // R, TWO * B // R
    M = XH * Z
    uw = W // R

    r = lax.axis_index("row")
    c = lax.axis_index("col")
    k = lax.rem(c, CORES)
    z = lax.rem(c // CORES, Z)
    xh = c // (CORES * Z)
    Y = R // XL
    y = r // XL
    xl = lax.rem(r, XL)

    def col_of(xh_, z_, k_):
        return (xh_ * Z + z_) * CORES + k_

    core_dev = (r, col_of(xh, z, 1 - k))
    x_dev = (r, col_of(1 - xh, z, k))
    cross_dev = (r, col_of(1 - xh, z, 1 - k))

    def z_at(i):
        return lax.rem(z + 1 + i, Z)

    def r_at(i):
        return lax.rem(r + 1 + i, R)

    def z_dev(zz):
        return (r, col_of(xh, zz, k))

    def row_dev(rr):
        return (rr, c)

    def rcopy(src, dst, ssem, rsem, dev):
        return pltpu.make_async_remote_copy(
            src_ref=src,
            dst_ref=dst,
            send_sem=ssem,
            recv_sem=rsem,
            device_id=dev,
            device_id_type=MESH,
        )

    def loop(n, body):
        def step(i, carry):
            body(i)
            return carry

        lax.fori_loop(0, n, step, 0)

    sel_copy = pltpu.make_async_copy(sel_any, sel, sem_sel.at[0])
    sel2_copy = pltpu.make_async_copy(sel2_any, sel2, sem_sel.at[1])
    sel_copy.start()
    sel2_copy.start()

    barrier = pltpu.get_barrier_semaphore()
    pl.semaphore_signal(barrier, inc=1, device_id=core_dev, device_id_type=MESH)
    pl.semaphore_signal(barrier, inc=1, device_id=x_dev, device_id_type=MESH)
    pl.semaphore_signal(barrier, inc=1, device_id=cross_dev, device_id_type=MESH)

    def greet_z(i):
        pl.semaphore_signal(barrier, inc=1, device_id=z_dev(z_at(i)), device_id_type=MESH)

    def greet_r(i):
        pl.semaphore_signal(barrier, inc=1, device_id=row_dev(r_at(i)), device_id_type=MESH)

    loop(Z - 1, greet_z)
    loop(R - 1, greet_r)

    for half in range(2):
        G[half, xh, z, k] = own_u[half]
        XG[half, y, xl] = own_x[half]

    pl.semaphore_wait(barrier, 3 + (Z - 1) + (R - 1))

    near = (y * XL + 1 - xl, c)

    def xgx(src_xl):
        return rcopy(XG.at[:, y, src_xl], XG.at[:, y, src_xl], xs_s.at[0], xs_r.at[0], near)

    def y_at(i):
        return lax.rem(y + 1 + i, Y)

    def xgy(src_y, to_y):
        return rcopy(
            XG.at[:, src_y], XG.at[:, src_y], xy_s.at[to_y], xy_r.at[src_y], (to_y * XL + xl, c)
        )

    far_p, far_m = Z // 2, Z // 2 - 1
    z_next = lax.rem(z + 1, Z)
    z_prev = lax.rem(z + Z - 1, Z)

    def behind(t):
        return lax.rem(z + Z - 1 - t, Z)

    def ahead(t):
        return lax.rem(z + 1 + t, Z)

    def a_ring(src_z, sems, to):
        block = G.at[0, xh, src_z, k]
        return rcopy(block, block, sems.at[src_z], a_r.at[src_z], z_dev(to))

    def b_ring(src_z, sems, to):
        block = G.at[1, :, src_z, k]
        return rcopy(block, block, sems.at[src_z], b_r.at[src_z], z_dev(to))

    def a_x(src_xh, src_z):
        block = G.at[0, src_xh, src_z, k]
        return rcopy(block, block, ax_s.at[src_z], ax_r.at[src_z], x_dev)

    def a_core(src_xh, src_z, src_k):
        block = G.at[0, src_xh, src_z, src_k]
        n = src_xh * Z + src_z
        return rcopy(block, block, ac_s.at[n], ac_r.at[n], core_dev)

    def b_core(src_z, src_k):
        block = G.at[1, :, src_z, src_k]
        return rcopy(block, block, bc_s.at[src_z], bc_r.at[src_z], core_dev)

    def b_x(src_xh):
        block = G.at[1, src_xh, z, k]
        return rcopy(block, block, bx_s.at[0], bx_r.at[0], x_dev)

    b_x(xh).start()
    xgx(xl).start()
    a_ring(z, ap_s, z_next).start()
    if far_m > 0:
        a_ring(z, am_s, z_prev).start()
    a_x(xh, z).start()
    a_core(xh, z, k).start()
    xgx(1 - xl).wait_recv()
    loop(Y - 1, lambda i: xgy(y, y_at(i)).start())
    b_x(1 - xh).wait_recv()
    b_ring(z, bp_s, z_next).start()
    if far_m > 0:
        b_ring(z, bm_s, z_prev).start()
    b_core(z, k).start()
    def a_step(t):
        zz = behind(t)
        a_ring(zz, ap_s, z_next).wait_recv()
        if t < far_p - 1:
            a_ring(zz, ap_s, z_next).start()
        a_x(xh, zz).start()
        a_core(xh, zz, k).start()
        if t < far_m:
            zz = ahead(t)
            a_ring(zz, am_s, z_prev).wait_recv()
            if t < far_m - 1:
                a_ring(zz, am_s, z_prev).start()
            a_x(xh, zz).start()
            a_core(xh, zz, k).start()

    def b_step(t):
        zz = behind(t)
        b_ring(zz, bp_s, z_next).wait_recv()
        if t < far_p - 1:
            b_ring(zz, bp_s, z_next).start()
        b_core(zz, k).start()
        if t < far_m:
            zz = ahead(t)
            b_ring(zz, bm_s, z_prev).wait_recv()
            if t < far_m - 1:
                b_ring(zz, bm_s, z_prev).start()
            b_core(zz, k).start()

    def cs(m):
        return rcopy(Pm.at[m, 1 - k], cr.at[m], cs_s.at[m], cs_r.at[m], core_dev)

    sel_copy.wait()
    sel2_copy.wait()

    def lower(m):
        first = sel[pl.ds(pl.multiple_of(m * (2 * s1), 16), 4 * s1), :]
        p1 = mm(first, X[:, 0:W])
        rows = sel2[pl.ds(pl.multiple_of(m * (2 * s2), 16), 4 * s2), :]
        p2 = mm(rows, X[:, W : 2 * W]) + mm(rows, X[:, 2 * W : 3 * W])
        for j in range(2):
            for core in range(CORES):
                n = 2 * j + core
                Pm[m + j, core, 0:s1, :] = p1[n * s1 : (n + 1) * s1]
                Pm[m + j, core, s1 : s1 + s2, :] = p2[n * s2 : (n + 1) * s2]
            cs(m + j).start()

    def pair_at(i):
        return 2 * lax.rem(z // 2 + 1 + i, Z // 2)

    def lower_at(n):
        lower(jnp.where(n < Z // 2, 1 - xh, xh) * Z + pair_at(lax.rem(n, Z // 2)))

    a_step(0)
    if far_p > 1:
        a_step(1)
    b_step(0)
    loop(Y - 1, lambda i: xgy(y_at(i), y).wait_recv())
    x1t = XG[0].reshape(W, ncol)
    lct = XG[1].reshape(W, ncol)
    clt = cl_ref[...].astype(F32).T.astype(BF16)
    x2 = (lct.astype(F32) - mm(clt, x1t)).T
    x2hi = x2.astype(BF16)
    X[:, 0:W] = x1t.astype(F32).T.astype(BF16)
    X[:, W : 2 * W] = x2hi
    X[:, 2 * W : 3 * W] = (x2 - x2hi.astype(F32)).astype(BF16)

    first = 0
    for t in range(1, far_p):
        if t + 1 < far_p:
            a_step(t + 1)
        share = Z // (2 * far_p)
        loop(share, lambda i, first=first: lower_at(first + i))
        first += share
        if t < far_p - 1:
            b_step(t)
            loop(share, lambda i, first=first: lower_at(first + i))
            first += share

    def over(i):
        zz = z_at(i)
        a_x(1 - xh, zz).wait_recv()
        a_core(1 - xh, zz, k).start()

    loop(Z, over)
    loop(Z - first, lambda i: lower_at(first + i))

    def rx(zz):
        return rcopy(xs.at[zz], xr.at[zz], rx_s.at[zz], rx_r.at[zz], x_dev)

    def rz(src_z, to_z):
        return rcopy(zs.at[to_z], zr.at[src_z], rz_s.at[to_z], rz_r.at[src_z], z_dev(to_z))

    def to_x(i):
        zz = z_at(i)
        m = (1 - xh) * Z + zz
        cs(m).wait_recv()
        xs[zz] = (Pm[m, k] + cr[m]).astype(BF16)
        rx(zz).start()

    loop(Z, to_x)

    def pu(j, src_r, to_r):
        return rcopy(
            PUb.at[j, to_r],
            ur_buf.at[j, src_r],
            pu_s.at[j, to_r],
            pu_r.at[j, src_r],
            row_dev(to_r),
        )

    loop(M, lambda i: a_core(i // Z, lax.rem(i, Z), 1 - k).wait_recv())
    PU[0] = mm(G[0].reshape(W, nb1 * B), sel[...])
    PUb[0] = PU[0].astype(BF16).reshape(R, uw, ncol)
    loop(R - 1, lambda i: pu(0, r, r_at(i)).start())

    if far_p > 1:
        b_step(far_p - 1)
    loop(Z, lambda i: b_core(i, 1 - k).wait_recv())
    cu = cu_ref[...]
    wide = 2 * B if nb1 % 2 == 0 else B

    def second(j):
        at = pl.ds(pl.multiple_of(j * wide, wide), wide)
        up = G[0, :, :, :, :, at].reshape(W, wide)
        uc = G[1, :, :, :, :, at].reshape(W, wide)
        v = uc.astype(F32) - mm(cu, up)
        hi = v.astype(BF16)
        V[0, :, at] = hi
        V[1, :, at] = (v - hi.astype(F32)).astype(BF16)

    loop(nb1 * B // wide, second)

    def both(j):
        PU[1 + j] = mm(V[j], sel[...])

    loop(2, both)
    PU[1] = PU[1] + PU[2]
    PUb[1] = PU[1].astype(BF16).reshape(R, uw, ncol)
    loop(R - 1, lambda i: pu(1, r, r_at(i)).start())

    def to_z(i):
        zz = z_at(i)
        m = xh * Z + zz
        cs(m).wait_recv()
        rx(zz).wait_recv()
        total = Pm[m, k] + cr[m] + xr[zz].astype(F32)

        @pl.when(i < Z - 1)
        def _():
            zs[zz] = total.astype(BF16)
            rz(z, zz).start()

        @pl.when(i == Z - 1)
        def _():
            own[...] = total

    loop(Z, to_z)


    tail[...] = dg2_ref[...] + exact(
        cu.astype(F32), exact(dg1_ref[...], cl_ref[...].astype(F32))
    )

    mine = pl.ds(pl.multiple_of(r * uw, 16), uw)

    def from_r(i):
        rr = r_at(i)
        for j in range(2):
            pu(j, rr, r).wait_recv()
            PU[j, mine, :] = PU[j, mine, :] + ur_buf[j, rr].astype(F32)

    loop(R - 1, from_r)
    u1 = (-PU[0, mine, :]).astype(BF16)
    u2 = (-PU[1, mine, :]).astype(BF16)
    dd[0] = mm(u1, X[:, 0:W])
    dd[1] = mm(u2, X[:, W : 2 * W]) + mm(u2, X[:, 2 * W : 3 * W])
    me = xh * CORES + k

    def d_four(src, half, to_, dev):
        return rcopy(dd.at[half], drc.at[src], d_s.at[to_], d_r.at[src], dev)

    core_at, x_at, cross_at = xh * CORES + 1 - k, (1 - xh) * CORES + k, (1 - xh) * CORES + 1 - k
    sends = (
        d_four(me, 1 - k, core_at, core_dev),
        d_four(me, k, x_at, x_dev),
        d_four(me, 1 - k, cross_at, cross_dev),
    )
    for send in sends:
        send.start()
    drc[me] = dd[k]
    u1_out[...] = u1
    u2_out[...] = mm(u2, pick_cols[...]).astype(BF16)

    for src in (core_at, x_at, cross_at):
        d_four(src, k, me, x_dev).wait_recv()
    dz[z] = ((drc[0] + drc[1]) + (drc[2] + drc[3])).astype(BF16)

    def dzc(src_z, to_z):
        return rcopy(dz.at[src_z], dz.at[src_z], dz_s.at[to_z], dz_r.at[src_z], z_dev(to_z))

    loop(Z - 1, lambda i: dzc(z, z_at(i)).start())
    loop(Z - 1, lambda i: dzc(z_at(i), z).wait_recv())
    total = dz[0].astype(F32)
    for i in range(1, Z):
        total = total + dz[i].astype(F32)
    Dall[k, r] = total

    def drow(src_r, to_r):
        return rcopy(
            Dall.at[k, src_r], Dall.at[k, src_r], dr_s.at[to_r], dr_r.at[src_r], row_dev(to_r)
        )

    def d_core(src_r, src_k):
        block = Dall.at[src_k, src_r]
        return rcopy(block, block, df_s.at[src_r], df_r.at[src_r], core_dev)

    loop(R - 1, lambda i: drow(r, r_at(i)).start())
    d_core(r, k).start()
    def from_z(i):
        zz = z_at(i)
        rz(zz, z).wait_recv()
        own[...] = own[...] + zr[zz].astype(F32)

    loop(Z - 1, from_z)
    l1_out[...] = (-own[0:s1, :]).astype(BF16)
    l2_out[...] = (-own[s1 : s1 + s2, :]).astype(BF16)


    def from_row(i):
        rr = r_at(i)
        drow(rr, r).wait_recv()
        d_core(rr, k).start()

    loop(R - 1, from_row)
    loop(R, lambda i: d_core(i, 1 - k).wait_recv())
    d1_out[...] = dg1_ref[...] - Dall[0].reshape(W, W)
    d2_out[...] = tail[...] - Dall[1].reshape(W, W)

    def left_z(i):
        zz = z_at(i)
        rz(z, zz).wait_send()
        dzc(z, zz).wait_send()

    def left_r(i):
        rr = r_at(i)
        pu(0, r, rr).wait_send()
        pu(1, r, rr).wait_send()
        drow(r, rr).wait_send()

    def left_x(i):
        a_x(xh, i).wait_send()
        rx(i).wait_send()
        b_core(i, k).wait_send()

    def left_c(i):
        a_core(i // Z, lax.rem(i, Z), k).wait_send()
        cs(i).wait_send()

    b_x(xh).wait_send()
    xgx(xl).wait_send()
    loop(Y - 1, lambda i: xgy(y, y_at(i)).wait_send())
    for t in range(far_p):
        a_ring(lax.rem(z + Z - t, Z), ap_s, z_next).wait_send()
        b_ring(lax.rem(z + Z - t, Z), bp_s, z_next).wait_send()
    for t in range(far_m):
        a_ring(lax.rem(z + t, Z), am_s, z_prev).wait_send()
        b_ring(lax.rem(z + t, Z), bm_s, z_prev).wait_send()
    loop(Z - 1, left_z)
    loop(R - 1, left_r)
    loop(Z, left_x)
    loop(M, left_c)
    loop(R, lambda i: d_core(i, k).wait_send())
    for send in sends:
        send.wait_send()


def pick(
    R,
    C,
    one_ref,
    two_ref,
    sep,
    lp_ref,
    lc_ref,
    up_ref,
    uc_ref,
    sel,
    sel2,
    own_u,
    own_x,
    pick_cols,
):
    r = lax.axis_index("row")
    c = lax.axis_index("col")
    runs = C // R
    nb1 = runs * ONE
    ur = up_ref.shape[0]
    lw = lp_ref.shape[0]

    def one_at(run, s):
        return one_ref[run * ONE + s]

    def two_at(run, t):
        return two_ref[run * TWO + t]

    def in_two(run, b):
        hit = (two_at(run, 0) == b).astype(jnp.int32)
        for t in range(1, TWO):
            hit = hit + (two_at(run, t) == b).astype(jnp.int32)
        return hit

    col_at = [pl.multiple_of((one_at(c, s) - c * SPAN) * B, B) for s in range(ONE)]

    def row_at(b):
        return pl.multiple_of((b - r * (runs * SPAN)) * B, B)

    def some_run(q, carry):
        run = r * runs + q
        for s in range(ONE):
            b = one_at(run, s)
            at = row_at(b)
            to = pl.ds(pl.multiple_of((q * ONE + s) * B, B), B)
            for t in range(ONE):
                sel[to, t * B : (t + 1) * B] = sep[pl.ds(at, B), pl.ds(col_at[t], B)]
            own_u[0, :, to] = up_ref[:, pl.ds(at, B)]
            piece = uc_ref[:, pl.ds(at, B)].astype(F32)
            hit = jnp.full((ur, B), in_two(run, b))
            own_u[1, :, to] = jnp.where(hit > 0, piece, 0.0).astype(BF16)
        for t in range(TWO):
            at = row_at(two_at(run, t))
            to = pl.ds(pl.multiple_of((q * TWO + t) * B, B), B)
            for s in range(ONE):
                sel2[to, s * B : (s + 1) * B] = sep[pl.ds(at, B), pl.ds(col_at[s], B)]
        return carry

    lax.fori_loop(0, runs, some_run, 0)

    same = lax.broadcasted_iota(jnp.int32, (B, B), 0) == lax.broadcasted_iota(jnp.int32, (B, B), 1)
    eye = jnp.where(same, 1.0, 0.0)
    for s in range(ONE):
        b = one_at(c, s)
        to = pl.ds(s * B, B)
        own_x[0, :, to] = lp_ref[:, pl.ds(col_at[s], B)]
        piece = lc_ref[:, pl.ds(col_at[s], B)].astype(F32)
        hit = jnp.full((lw, B), in_two(c, b))
        own_x[1, :, to] = jnp.where(hit > 0, piece, 0.0).astype(BF16)
        for t in range(TWO):
            hit = jnp.full((B, B), (two_at(c, t) == b).astype(jnp.int32))
            pick_cols[to, t * B : (t + 1) * B] = jnp.where(hit > 0, eye, 0.0).astype(BF16)


def on_device(
    R,
    C,
    inv_sep,
    lower_one,
    upper_one,
    diag_inv_one,
    blocks_one,
    lower_two,
    upper_two,
    corner_lower,
    corner_upper,
    diag_inv_two,
    blocks_two,
):
    W = diag_inv_one.shape[0]
    Z = C // (XH * CORES)
    M = XH * Z
    runs = C // R
    nb1 = runs * ONE
    ncol = ONE * B
    ur, lw, uw = W // C, W // R, W // R
    s1, s2 = ONE * B // R, TWO * B // R
    sh = s1 + s2
    vmem = pl.BlockSpec(memory_space=pltpu.VMEM)
    smem = pl.BlockSpec(memory_space=pltpu.SMEM)
    dma = pltpu.SemaphoreType.DMA
    picked = pl.pallas_call(
        functools.partial(pick, R, C),
        out_shape=(
            jax.ShapeDtypeStruct((nb1 * B, ncol), BF16),
            jax.ShapeDtypeStruct((runs * TWO * B, ncol), BF16),
            jax.ShapeDtypeStruct((2, ur, nb1 * B), BF16),
            jax.ShapeDtypeStruct((2, lw, ncol), BF16),
            jax.ShapeDtypeStruct((ncol, TWO * B), BF16),
        ),
        in_specs=[smem, smem] + [vmem] * 5,
        out_specs=(vmem,) * 5,
        compiler_params=pltpu.CompilerParams(vmem_limit_bytes=24 * 2**20),
        name="pick",
    )(blocks_one, blocks_two, inv_sep, lower_one.T, lower_two.T, upper_one, upper_two)
    return pl.pallas_call(
        functools.partial(kernel, R, C, W),
        out_shape=(
            jax.ShapeDtypeStruct((s1, W), BF16),
            jax.ShapeDtypeStruct((uw, ncol), BF16),
            jax.ShapeDtypeStruct((W, W), F32),
            jax.ShapeDtypeStruct((s2, W), BF16),
            jax.ShapeDtypeStruct((uw, TWO * B), BF16),
            jax.ShapeDtypeStruct((W, W), F32),
        ),
        in_specs=[pl.BlockSpec(memory_space=pl.ANY)] * 2 + [vmem] * 7,
        out_specs=(vmem,) * 6,
        scratch_shapes=[
            pltpu.VMEM((nb1 * B, ncol), BF16),
            pltpu.VMEM((runs * TWO * B, ncol), BF16),
            pltpu.VMEM((2, XH, Z, CORES, ur, nb1 * B), BF16),
            pltpu.VMEM((2, W, nb1 * B), BF16),
            pltpu.VMEM((2, R // XL, XL, lw, ncol), BF16),
            pltpu.VMEM((ncol, 3 * W), BF16),
            pltpu.VMEM((M, 2, sh, W), F32),
            pltpu.VMEM((M, sh, W), F32),
            pltpu.VMEM((Z, sh, W), BF16),
            pltpu.VMEM((Z, sh, W), BF16),
            pltpu.VMEM((Z, sh, W), BF16),
            pltpu.VMEM((Z, sh, W), BF16),
            pltpu.VMEM((sh, W), F32),
            pltpu.VMEM((3, W, ncol), F32),
            pltpu.VMEM((2, R, uw, ncol), BF16),
            pltpu.VMEM((2, R, uw, ncol), BF16),
            pltpu.VMEM((2, uw, W), F32),
            pltpu.VMEM((XH * CORES, uw, W), F32),
            pltpu.VMEM((Z, uw, W), BF16),
            pltpu.VMEM((2, R, uw, W), F32),
            pltpu.VMEM((W, W), F32),
        ]
        + [dma((n,)) for n in (2, 1, 1, R // XL, R // XL)]
        + [dma((n,)) for n in (Z, Z, Z, Z, Z, Z, Z, Z, M, M, Z, Z, 1, 1)]
        + [dma((n,)) for n in (M, M, Z, Z, Z, Z)]
        + [dma((2, R)), dma((2, R))]
        + [dma((n,)) for n in (4, 4, Z, Z, R, R, R, R)],
        compiler_params=pltpu.CompilerParams(
            collective_id=0, has_side_effects=True, vmem_limit_bytes=40 * 2**20
        ),
        name="panels",
    )(*picked, corner_lower, corner_upper, diag_inv_one, diag_inv_two)


def solution(mesh):
    R, C = mesh.shape["row"], mesh.shape["col"]
    return jax.shard_map(
        functools.partial(on_device, R, C),
        mesh=mesh,
        in_specs=(
            P("row", "col"),
            P("col", "row"),
            P("col", "row"),
            P(),
            P(),
            P("col", "row"),
            P("col", "row"),
            P(),
            P(),
            P(),
            P(),
        ),
        out_specs=(
            P(("row", "col"), None),
            P("row", "col"),
            P(),
            P(("row", "col"), None),
            P("row", "col"),
            P(),
        ),
        check_vma=False,
    )
```

```python
import functools

import jax
import jax.numpy as jnp
from jax import lax
from jax.experimental import pallas as pl
from jax.experimental.pallas import tpu as pltpu
from jax.sharding import PartitionSpec as P

B = 128
SPAN = 6
ONE = 5
TWO = 4
XH = 2
CORES = 2
XL = 2
MESH = pl.DeviceIdType.MESH
F32 = jnp.float32
BF16 = jnp.bfloat16


def mm(a, b):
    return jnp.dot(a, b, preferred_element_type=F32)


def exact(a, b):
    return jnp.dot(
        a, b, preferred_element_type=F32, precision=lax.Precision.HIGHEST
    )


def kernel(
    R,
    C,
    W,
    sel_any,
    sel2_any,
    own_u,
    own_x,
    pick_cols,
    cl_ref,
    cu_ref,
    dg1_ref,
    dg2_ref,
    l1_out,
    u1_out,
    d1_out,
    l2_out,
    u2_out,
    d2_out,
    sel,
    sel2,
    G,
    V,
    XG,
    X,
    Pm,
    cr,
    xs,
    xr,
    zs,
    zr,
    own,
    PU,
    PUb,
    ur_buf,
    dd,
    drc,
    dz,
    Dall,
    tail,
    sem_sel,
    xs_s,
    xs_r,
    xy_s,
    xy_r,
    ap_s,
    am_s,
    a_r,
    bp_s,
    bm_s,
    b_r,
    ax_s,
    ax_r,
    ac_s,
    ac_r,
    bc_s,
    bc_r,
    bx_s,
    bx_r,
    cs_s,
    cs_r,
    rx_s,
    rx_r,
    rz_s,
    rz_r,
    pu_s,
    pu_r,
    d_s,
    d_r,
    dz_s,
    dz_r,
    dr_s,
    dr_r,
    df_s,
    df_r,
):
    Z = C // (XH * CORES)
    runs = C // R
    nb1, nb2 = runs * ONE, runs * TWO
    ncol = ONE * B
    ur = W // C
    lw = W // R
    s1, s2 = ONE * B // R, TWO * B // R
    M = XH * Z
    uw = W // R

    r = lax.axis_index("row")
    c = lax.axis_index("col")
    k = lax.rem(c, CORES)
    z = lax.rem(c // CORES, Z)
    xh = c // (CORES * Z)
    Y = R // XL
    y = r // XL
    xl = lax.rem(r, XL)

    def col_of(xh_, z_, k_):
        return (xh_ * Z + z_) * CORES + k_

    core_dev = (r, col_of(xh, z, 1 - k))
    x_dev = (r, col_of(1 - xh, z, k))
    cross_dev = (r, col_of(1 - xh, z, 1 - k))

    def z_at(i):
        return lax.rem(z + 1 + i, Z)

    def r_at(i):
        return lax.rem(r + 1 + i, R)

    def z_dev(zz):
        return (r, col_of(xh, zz, k))

    def row_dev(rr):
        return (rr, c)

    def rcopy(src, dst, ssem, rsem, dev):
        return pltpu.make_async_remote_copy(
            src_ref=src,
            dst_ref=dst,
            send_sem=ssem,
            recv_sem=rsem,
            device_id=dev,
            device_id_type=MESH,
        )

    def loop(n, body):
        def step(i, carry):
            body(i)
            return carry

        lax.fori_loop(0, n, step, 0)

    sel_copy = pltpu.make_async_copy(sel_any, sel, sem_sel.at[0])
    sel2_copy = pltpu.make_async_copy(sel2_any, sel2, sem_sel.at[1])
    sel_copy.start()
    sel2_copy.start()

    barrier = pltpu.get_barrier_semaphore()
    pl.semaphore_signal(barrier, inc=1, device_id=core_dev, device_id_type=MESH)
    pl.semaphore_signal(barrier, inc=1, device_id=x_dev, device_id_type=MESH)
    pl.semaphore_signal(barrier, inc=1, device_id=cross_dev, device_id_type=MESH)

    def greet_z(i):
        pl.semaphore_signal(barrier, inc=1, device_id=z_dev(z_at(i)), device_id_type=MESH)

    def greet_r(i):
        pl.semaphore_signal(barrier, inc=1, device_id=row_dev(r_at(i)), device_id_type=MESH)

    loop(Z - 1, greet_z)
    loop(R - 1, greet_r)

    for half in range(2):
        G[half, xh, z, k] = own_u[half]
        XG[half, y, xl] = own_x[half]

    pl.semaphore_wait(barrier, 3 + (Z - 1) + (R - 1))

    near = (y * XL + 1 - xl, c)

    def xgx(src_xl):
        return rcopy(XG.at[:, y, src_xl], XG.at[:, y, src_xl], xs_s.at[0], xs_r.at[0], near)

    def y_at(i):
        return lax.rem(y + 1 + i, Y)

    def xgy(src_y, to_y):
        return rcopy(
            XG.at[:, src_y], XG.at[:, src_y], xy_s.at[to_y], xy_r.at[src_y], (to_y * XL + xl, c)
        )

    far_p, far_m = Z // 2, Z // 2 - 1
    z_next = lax.rem(z + 1, Z)
    z_prev = lax.rem(z + Z - 1, Z)

    def behind(t):
        return lax.rem(z + Z - 1 - t, Z)

    def ahead(t):
        return lax.rem(z + 1 + t, Z)

    def a_ring(src_z, sems, to):
        block = G.at[0, xh, src_z, k]
        return rcopy(block, block, sems.at[src_z], a_r.at[src_z], z_dev(to))

    def b_ring(src_z, sems, to):
        block = G.at[1, :, src_z, k]
        return rcopy(block, block, sems.at[src_z], b_r.at[src_z], z_dev(to))

    def a_x(src_xh, src_z):
        block = G.at[0, src_xh, src_z, k]
        return rcopy(block, block, ax_s.at[src_z], ax_r.at[src_z], x_dev)

    def a_core(src_xh, src_z, src_k):
        block = G.at[0, src_xh, src_z, src_k]
        n = src_xh * Z + src_z
        return rcopy(block, block, ac_s.at[n], ac_r.at[n], core_dev)

    def b_core(src_z, src_k):
        block = G.at[1, :, src_z, src_k]
        return rcopy(block, block, bc_s.at[src_z], bc_r.at[src_z], core_dev)

    def b_x(src_xh):
        block = G.at[1, src_xh, z, k]
        return rcopy(block, block, bx_s.at[0], bx_r.at[0], x_dev)

    b_x(xh).start()
    xgx(xl).start()
    a_ring(z, ap_s, z_next).start()
    if far_m > 0:
        a_ring(z, am_s, z_prev).start()
    a_x(xh, z).start()
    a_core(xh, z, k).start()
    xgx(1 - xl).wait_recv()
    loop(Y - 1, lambda i: xgy(y, y_at(i)).start())
    b_x(1 - xh).wait_recv()
    b_ring(z, bp_s, z_next).start()
    if far_m > 0:
        b_ring(z, bm_s, z_prev).start()
    b_core(z, k).start()
    def a_step(t):
        zz = behind(t)
        a_ring(zz, ap_s, z_next).wait_recv()
        if t < far_p - 1:
            a_ring(zz, ap_s, z_next).start()
        a_x(xh, zz).start()
        a_core(xh, zz, k).start()
        if t < far_m:
            zz = ahead(t)
            a_ring(zz, am_s, z_prev).wait_recv()
            if t < far_m - 1:
                a_ring(zz, am_s, z_prev).start()
            a_x(xh, zz).start()
            a_core(xh, zz, k).start()

    def b_step(t):
        zz = behind(t)
        b_ring(zz, bp_s, z_next).wait_recv()
        if t < far_p - 1:
            b_ring(zz, bp_s, z_next).start()
        b_core(zz, k).start()
        if t < far_m:
            zz = ahead(t)
            b_ring(zz, bm_s, z_prev).wait_recv()
            if t < far_m - 1:
                b_ring(zz, bm_s, z_prev).start()
            b_core(zz, k).start()

    def cs(m):
        return rcopy(Pm.at[m, 1 - k], cr.at[m], cs_s.at[m], cs_r.at[m], core_dev)

    sel_copy.wait()
    sel2_copy.wait()

    def lower(m):
        first = sel[pl.ds(pl.multiple_of(m * (2 * s1), 16), 4 * s1), :]
        p1 = mm(first, X[:, 0:W])
        rows = sel2[pl.ds(pl.multiple_of(m * (2 * s2), 16), 4 * s2), :]
        p2 = mm(rows, X[:, W : 2 * W]) + mm(rows, X[:, 2 * W : 3 * W])
        for j in range(2):
            for core in range(CORES):
                n = 2 * j + core
                Pm[m + j, core, 0:s1, :] = p1[n * s1 : (n + 1) * s1]
                Pm[m + j, core, s1 : s1 + s2, :] = p2[n * s2 : (n + 1) * s2]
            cs(m + j).start()

    def pair_at(i):
        return 2 * lax.rem(z // 2 + 1 + i, Z // 2)

    def lower_at(n):
        lower(jnp.where(n < Z // 2, 1 - xh, xh) * Z + pair_at(lax.rem(n, Z // 2)))

    a_step(0)
    for t in range(1, far_p):
        a_step(t)
        b_step(t - 1)
    loop(Y - 1, lambda i: xgy(y_at(i), y).wait_recv())
    x1t = XG[0].reshape(W, ncol)
    lct = XG[1].reshape(W, ncol)
    clt = cl_ref[...].astype(F32).T.astype(BF16)
    x2 = (lct.astype(F32) - mm(clt, x1t)).T
    x2hi = x2.astype(BF16)
    X[:, 0:W] = x1t.astype(F32).T.astype(BF16)
    X[:, W : 2 * W] = x2hi
    X[:, 2 * W : 3 * W] = (x2 - x2hi.astype(F32)).astype(BF16)

    loop(Z // 2, lower_at)

    def over(i):
        zz = z_at(i)
        a_x(1 - xh, zz).wait_recv()
        a_core(1 - xh, zz, k).start()

    loop(Z, over)
    loop(Z // 2, lambda i: lower_at(Z // 2 + i))

    def rx(zz):
        return rcopy(xs.at[zz], xr.at[zz], rx_s.at[zz], rx_r.at[zz], x_dev)

    def rz(src_z, to_z):
        return rcopy(zs.at[to_z], zr.at[src_z], rz_s.at[to_z], rz_r.at[src_z], z_dev(to_z))

    def to_x(i):
        zz = z_at(i)
        m = (1 - xh) * Z + zz
        cs(m).wait_recv()
        xs[zz] = (Pm[m, k] + cr[m]).astype(BF16)
        rx(zz).start()

    loop(Z, to_x)

    def pu(j, src_r, to_r):
        return rcopy(
            PUb.at[j, to_r],
            ur_buf.at[j, src_r],
            pu_s.at[j, to_r],
            pu_r.at[j, src_r],
            row_dev(to_r),
        )

    loop(M, lambda i: a_core(i // Z, lax.rem(i, Z), 1 - k).wait_recv())
    PU[0] = mm(G[0].reshape(W, nb1 * B), sel[...])
    PUb[0] = PU[0].astype(BF16).reshape(R, uw, ncol)
    loop(R - 1, lambda i: pu(0, r, r_at(i)).start())

    b_step(far_p - 1)
    loop(Z, lambda i: b_core(i, 1 - k).wait_recv())
    cu = cu_ref[...]
    wide = 2 * B if nb1 % 2 == 0 else B

    def second(j):
        at = pl.ds(pl.multiple_of(j * wide, wide), wide)
        up = G[0, :, :, :, :, at].reshape(W, wide)
        uc = G[1, :, :, :, :, at].reshape(W, wide)
        v = uc.astype(F32) - mm(cu, up)
        hi = v.astype(BF16)
        V[0, :, at] = hi
        V[1, :, at] = (v - hi.astype(F32)).astype(BF16)

    loop(nb1 * B // wide, second)

    def both(j):
        PU[1 + j] = mm(V[j], sel[...])

    loop(2, both)
    PU[1] = PU[1] + PU[2]
    PUb[1] = PU[1].astype(BF16).reshape(R, uw, ncol)
    loop(R - 1, lambda i: pu(1, r, r_at(i)).start())

    def to_z(i):
        zz = z_at(i)
        m = xh * Z + zz
        cs(m).wait_recv()
        rx(zz).wait_recv()
        total = Pm[m, k] + cr[m] + xr[zz].astype(F32)

        @pl.when(i < Z - 1)
        def _():
            zs[zz] = total.astype(BF16)
            rz(z, zz).start()

        @pl.when(i == Z - 1)
        def _():
            own[...] = total

    loop(Z, to_z)


    tail[...] = dg2_ref[...] + exact(
        cu.astype(F32), exact(dg1_ref[...], cl_ref[...].astype(F32))
    )

    mine = pl.ds(pl.multiple_of(r * uw, 16), uw)

    def from_r(i):
        rr = r_at(i)
        for j in range(2):
            pu(j, rr, r).wait_recv()
            PU[j, mine, :] = PU[j, mine, :] + ur_buf[j, rr].astype(F32)

    loop(R - 1, from_r)
    u1 = (-PU[0, mine, :]).astype(BF16)
    u2 = (-PU[1, mine, :]).astype(BF16)
    dd[0] = mm(u1, X[:, 0:W])
    dd[1] = mm(u2, X[:, W : 2 * W]) + mm(u2, X[:, 2 * W : 3 * W])
    me = xh * CORES + k

    def d_four(src, half, to_, dev):
        return rcopy(dd.at[half], drc.at[src], d_s.at[to_], d_r.at[src], dev)

    core_at, x_at, cross_at = xh * CORES + 1 - k, (1 - xh) * CORES + k, (1 - xh) * CORES + 1 - k
    sends = (
        d_four(me, 1 - k, core_at, core_dev),
        d_four(me, k, x_at, x_dev),
        d_four(me, 1 - k, cross_at, cross_dev),
    )
    for send in sends:
        send.start()
    drc[me] = dd[k]
    u1_out[...] = u1
    u2_out[...] = mm(u2, pick_cols[...]).astype(BF16)

    for src in (core_at, x_at, cross_at):
        d_four(src, k, me, x_dev).wait_recv()
    dz[z] = ((drc[0] + drc[1]) + (drc[2] + drc[3])).astype(BF16)

    def dzc(src_z, to_z):
        return rcopy(dz.at[src_z], dz.at[src_z], dz_s.at[to_z], dz_r.at[src_z], z_dev(to_z))

    loop(Z - 1, lambda i: dzc(z, z_at(i)).start())
    loop(Z - 1, lambda i: dzc(z_at(i), z).wait_recv())
    total = dz[0].astype(F32)
    for i in range(1, Z):
        total = total + dz[i].astype(F32)
    Dall[k, r] = total

    def drow(src_r, to_r):
        return rcopy(
            Dall.at[k, src_r], Dall.at[k, src_r], dr_s.at[to_r], dr_r.at[src_r], row_dev(to_r)
        )

    def d_core(src_r, src_k):
        block = Dall.at[src_k, src_r]
        return rcopy(block, block, df_s.at[src_r], df_r.at[src_r], core_dev)

    loop(R - 1, lambda i: drow(r, r_at(i)).start())
    d_core(r, k).start()
    def from_z(i):
        zz = z_at(i)
        rz(zz, z).wait_recv()
        own[...] = own[...] + zr[zz].astype(F32)

    loop(Z - 1, from_z)
    l1_out[...] = (-own[0:s1, :]).astype(BF16)
    l2_out[...] = (-own[s1 : s1 + s2, :]).astype(BF16)


    def from_row(i):
        rr = r_at(i)
        drow(rr, r).wait_recv()
        d_core(rr, k).start()

    loop(R - 1, from_row)
    loop(R, lambda i: d_core(i, 1 - k).wait_recv())
    d1_out[...] = dg1_ref[...] - Dall[0].reshape(W, W)
    d2_out[...] = tail[...] - Dall[1].reshape(W, W)

    def left_z(i):
        zz = z_at(i)
        rz(z, zz).wait_send()
        dzc(z, zz).wait_send()

    def left_r(i):
        rr = r_at(i)
        pu(0, r, rr).wait_send()
        pu(1, r, rr).wait_send()
        drow(r, rr).wait_send()

    def left_x(i):
        a_x(xh, i).wait_send()
        rx(i).wait_send()
        b_core(i, k).wait_send()

    def left_c(i):
        a_core(i // Z, lax.rem(i, Z), k).wait_send()
        cs(i).wait_send()

    b_x(xh).wait_send()
    xgx(xl).wait_send()
    loop(Y - 1, lambda i: xgy(y, y_at(i)).wait_send())
    for t in range(far_p):
        a_ring(lax.rem(z + Z - t, Z), ap_s, z_next).wait_send()
        b_ring(lax.rem(z + Z - t, Z), bp_s, z_next).wait_send()
    for t in range(far_m):
        a_ring(lax.rem(z + t, Z), am_s, z_prev).wait_send()
        b_ring(lax.rem(z + t, Z), bm_s, z_prev).wait_send()
    loop(Z - 1, left_z)
    loop(R - 1, left_r)
    loop(Z, left_x)
    loop(M, left_c)
    loop(R, lambda i: d_core(i, k).wait_send())
    for send in sends:
        send.wait_send()


def pick(
    R,
    C,
    one_ref,
    two_ref,
    sep,
    lp_ref,
    lc_ref,
    up_ref,
    uc_ref,
    sel,
    sel2,
    own_u,
    own_x,
    pick_cols,
):
    r = lax.axis_index("row")
    c = lax.axis_index("col")
    runs = C // R
    nb1 = runs * ONE
    ur = up_ref.shape[0]
    lw = lp_ref.shape[0]

    def one_at(run, s):
        return one_ref[run * ONE + s]

    def two_at(run, t):
        return two_ref[run * TWO + t]

    def in_two(run, b):
        hit = (two_at(run, 0) == b).astype(jnp.int32)
        for t in range(1, TWO):
            hit = hit + (two_at(run, t) == b).astype(jnp.int32)
        return hit

    col_at = [pl.multiple_of((one_at(c, s) - c * SPAN) * B, B) for s in range(ONE)]

    def row_at(b):
        return pl.multiple_of((b - r * (runs * SPAN)) * B, B)

    def some_run(q, carry):
        run = r * runs + q
        for s in range(ONE):
            b = one_at(run, s)
            at = row_at(b)
            to = pl.ds(pl.multiple_of((q * ONE + s) * B, B), B)
            for t in range(ONE):
                sel[to, t * B : (t + 1) * B] = sep[pl.ds(at, B), pl.ds(col_at[t], B)]
            own_u[0, :, to] = up_ref[:, pl.ds(at, B)]
            piece = uc_ref[:, pl.ds(at, B)].astype(F32)
            hit = jnp.full((ur, B), in_two(run, b))
            own_u[1, :, to] = jnp.where(hit > 0, piece, 0.0).astype(BF16)
        for t in range(TWO):
            at = row_at(two_at(run, t))
            to = pl.ds(pl.multiple_of((q * TWO + t) * B, B), B)
            for s in range(ONE):
                sel2[to, s * B : (s + 1) * B] = sep[pl.ds(at, B), pl.ds(col_at[s], B)]
        return carry

    lax.fori_loop(0, runs, some_run, 0)

    same = lax.broadcasted_iota(jnp.int32, (B, B), 0) == lax.broadcasted_iota(jnp.int32, (B, B), 1)
    eye = jnp.where(same, 1.0, 0.0)
    for s in range(ONE):
        b = one_at(c, s)
        to = pl.ds(s * B, B)
        own_x[0, :, to] = lp_ref[:, pl.ds(col_at[s], B)]
        piece = lc_ref[:, pl.ds(col_at[s], B)].astype(F32)
        hit = jnp.full((lw, B), in_two(c, b))
        own_x[1, :, to] = jnp.where(hit > 0, piece, 0.0).astype(BF16)
        for t in range(TWO):
            hit = jnp.full((B, B), (two_at(c, t) == b).astype(jnp.int32))
            pick_cols[to, t * B : (t + 1) * B] = jnp.where(hit > 0, eye, 0.0).astype(BF16)


def hand_over(*refs):
    n = (len(refs) - 1) // 2
    copies = [pltpu.make_async_copy(refs[i], refs[n + i], refs[-1].at[i]) for i in range(n)]
    for copy in copies:
        copy.start()
    for copy in copies:
        copy.wait()


def on_device(
    R,
    C,
    inv_sep,
    lower_one,
    upper_one,
    diag_inv_one,
    blocks_one,
    lower_two,
    upper_two,
    corner_lower,
    corner_upper,
    diag_inv_two,
    blocks_two,
):
    W = diag_inv_one.shape[0]
    Z = C // (XH * CORES)
    M = XH * Z
    runs = C // R
    nb1 = runs * ONE
    ncol = ONE * B
    ur, lw, uw = W // C, W // R, W // R
    s1, s2 = ONE * B // R, TWO * B // R
    sh = s1 + s2
    vmem = pl.BlockSpec(memory_space=pltpu.VMEM)
    hbm = pl.BlockSpec(memory_space=pltpu.HBM)
    smem = pl.BlockSpec(memory_space=pltpu.SMEM)
    dma = pltpu.SemaphoreType.DMA
    picked = pl.pallas_call(
        functools.partial(pick, R, C),
        out_shape=(
            jax.ShapeDtypeStruct((nb1 * B, ncol), BF16),
            jax.ShapeDtypeStruct((runs * TWO * B, ncol), BF16),
            jax.ShapeDtypeStruct((2, ur, nb1 * B), BF16),
            jax.ShapeDtypeStruct((2, lw, ncol), BF16),
            jax.ShapeDtypeStruct((ncol, TWO * B), BF16),
        ),
        in_specs=[smem, smem] + [vmem] * 5,
        out_specs=(vmem,) * 5,
        compiler_params=pltpu.CompilerParams(vmem_limit_bytes=24 * 2**20),
        name="pick",
    )(blocks_one, blocks_two, inv_sep, lower_one.T, lower_two.T, upper_one, upper_two)
    results = pl.pallas_call(
        functools.partial(kernel, R, C, W),
        out_shape=(
            jax.ShapeDtypeStruct((s1, W), BF16),
            jax.ShapeDtypeStruct((uw, ncol), BF16),
            jax.ShapeDtypeStruct((W, W), F32),
            jax.ShapeDtypeStruct((s2, W), BF16),
            jax.ShapeDtypeStruct((uw, TWO * B), BF16),
            jax.ShapeDtypeStruct((W, W), F32),
        ),
        in_specs=[pl.BlockSpec(memory_space=pl.ANY)] * 2 + [vmem] * 7,
        out_specs=(vmem,) * 6,
        scratch_shapes=[
            pltpu.VMEM((nb1 * B, ncol), BF16),
            pltpu.VMEM((runs * TWO * B, ncol), BF16),
            pltpu.VMEM((2, XH, Z, CORES, ur, nb1 * B), BF16),
            pltpu.VMEM((2, W, nb1 * B), BF16),
            pltpu.VMEM((2, R // XL, XL, lw, ncol), BF16),
            pltpu.VMEM((ncol, 3 * W), BF16),
            pltpu.VMEM((M, 2, sh, W), F32),
            pltpu.VMEM((M, sh, W), F32),
            pltpu.VMEM((Z, sh, W), BF16),
            pltpu.VMEM((Z, sh, W), BF16),
            pltpu.VMEM((Z, sh, W), BF16),
            pltpu.VMEM((Z, sh, W), BF16),
            pltpu.VMEM((sh, W), F32),
            pltpu.VMEM((3, W, ncol), F32),
            pltpu.VMEM((2, R, uw, ncol), BF16),
            pltpu.VMEM((2, R, uw, ncol), BF16),
            pltpu.VMEM((2, uw, W), F32),
            pltpu.VMEM((XH * CORES, uw, W), F32),
            pltpu.VMEM((Z, uw, W), BF16),
            pltpu.VMEM((2, R, uw, W), F32),
            pltpu.VMEM((W, W), F32),
        ]
        + [dma((n,)) for n in (2, 1, 1, R // XL, R // XL)]
        + [dma((n,)) for n in (Z, Z, Z, Z, Z, Z, Z, Z, M, M, Z, Z, 1, 1)]
        + [dma((n,)) for n in (M, M, Z, Z, Z, Z)]
        + [dma((2, R)), dma((2, R))]
        + [dma((n,)) for n in (4, 4, Z, Z, R, R, R, R)],
        compiler_params=pltpu.CompilerParams(
            collective_id=0, has_side_effects=True, vmem_limit_bytes=40 * 2**20
        ),
        name="panels",
    )(*picked, corner_lower, corner_upper, diag_inv_one, diag_inv_two)
    return pl.pallas_call(
        hand_over,
        out_shape=tuple(jax.ShapeDtypeStruct(a.shape, a.dtype) for a in results),
        in_specs=[vmem] * len(results),
        out_specs=(hbm,) * len(results),
        scratch_shapes=[dma((len(results),))],
        compiler_params=pltpu.CompilerParams(vmem_limit_bytes=4 * 2**20),
        name="hand_over",
    )(*results)


def solution(mesh):
    R, C = mesh.shape["row"], mesh.shape["col"]
    return jax.shard_map(
        functools.partial(on_device, R, C),
        mesh=mesh,
        in_specs=(
            P("row", "col"),
            P("col", "row"),
            P("col", "row"),
            P(),
            P(),
            P("col", "row"),
            P("col", "row"),
            P(),
            P(),
            P(),
            P(),
        ),
        out_specs=(
            P(("row", "col"), None),
            P("row", "col"),
            P(),
            P(("row", "col"), None),
            P("row", "col"),
            P(),
        ),
        check_vma=False,
    )
```

```python
import functools

import jax
import jax.numpy as jnp
from jax import lax
from jax.experimental import pallas as pl
from jax.experimental.pallas import tpu as pltpu
from jax.sharding import PartitionSpec as P

B = 128
SPAN = 6
ONE = 5
TWO = 4
XH = 2
CORES = 2
XL = 2
MESH = pl.DeviceIdType.MESH
F32 = jnp.float32
BF16 = jnp.bfloat16


def mm(a, b):
    return jnp.dot(a, b, preferred_element_type=F32)


def exact(a, b):
    return jnp.dot(
        a, b, preferred_element_type=F32, precision=lax.Precision.HIGHEST
    )


def kernel(
    R,
    C,
    W,
    sel_any,
    sel2_any,
    own_u,
    own_x,
    pick_cols,
    cl_ref,
    cu_ref,
    dg1_ref,
    dg2_ref,
    l1_out,
    u1_out,
    d1_out,
    l2_out,
    u2_out,
    d2_out,
    sel,
    sel2,
    G,
    V,
    XG,
    X,
    Pm,
    cr,
    xs,
    xr,
    zs,
    zr,
    own,
    PU,
    PUb,
    ur_buf,
    dd,
    drc,
    dz,
    Dall,
    tail,
    sem_sel,
    xs_s,
    xs_r,
    xy_s,
    xy_r,
    ap_s,
    am_s,
    a_r,
    bp_s,
    bm_s,
    b_r,
    ax_s,
    ax_r,
    ac_s,
    ac_r,
    bc_s,
    bc_r,
    bx_s,
    bx_r,
    cs_s,
    cs_r,
    rx_s,
    rx_r,
    rz_s,
    rz_r,
    pu_s,
    pu_r,
    d_s,
    d_r,
    dz_s,
    dz_r,
    dr_s,
    dr_r,
    df_s,
    df_r,
):
    Z = C // (XH * CORES)
    runs = C // R
    nb1, nb2 = runs * ONE, runs * TWO
    ncol = ONE * B
    ur = W // C
    lw = W // R
    s1, s2 = ONE * B // R, TWO * B // R
    M = XH * Z
    uw = W // R

    r = lax.axis_index("row")
    c = lax.axis_index("col")
    k = lax.rem(c, CORES)
    z = lax.rem(c // CORES, Z)
    xh = c // (CORES * Z)
    Y = R // XL
    y = r // XL
    xl = lax.rem(r, XL)

    def col_of(xh_, z_, k_):
        return (xh_ * Z + z_) * CORES + k_

    core_dev = (r, col_of(xh, z, 1 - k))
    x_dev = (r, col_of(1 - xh, z, k))
    cross_dev = (r, col_of(1 - xh, z, 1 - k))

    def z_at(i):
        return lax.rem(z + 1 + i, Z)

    def r_at(i):
        return lax.rem(r + 1 + i, R)

    def z_dev(zz):
        return (r, col_of(xh, zz, k))

    def row_dev(rr):
        return (rr, c)

    def rcopy(src, dst, ssem, rsem, dev):
        return pltpu.make_async_remote_copy(
            src_ref=src,
            dst_ref=dst,
            send_sem=ssem,
            recv_sem=rsem,
            device_id=dev,
            device_id_type=MESH,
        )

    def loop(n, body):
        def step(i, carry):
            body(i)
            return carry

        lax.fori_loop(0, n, step, 0)

    sel_copy = pltpu.make_async_copy(sel_any, sel, sem_sel.at[0])
    sel2_copy = pltpu.make_async_copy(sel2_any, sel2, sem_sel.at[1])
    sel_copy.start()
    sel2_copy.start()

    barrier = pltpu.get_barrier_semaphore()
    pl.semaphore_signal(barrier, inc=1, device_id=core_dev, device_id_type=MESH)
    pl.semaphore_signal(barrier, inc=1, device_id=x_dev, device_id_type=MESH)
    pl.semaphore_signal(barrier, inc=1, device_id=cross_dev, device_id_type=MESH)

    def greet_z(i):
        pl.semaphore_signal(barrier, inc=1, device_id=z_dev(z_at(i)), device_id_type=MESH)

    def greet_r(i):
        pl.semaphore_signal(barrier, inc=1, device_id=row_dev(r_at(i)), device_id_type=MESH)

    loop(Z - 1, greet_z)
    loop(R - 1, greet_r)

    for half in range(2):
        G[half, xh, z, k] = own_u[half]
        XG[half, y, xl] = own_x[half]

    pl.semaphore_wait(barrier, 3 + (Z - 1) + (R - 1))

    near = (y * XL + 1 - xl, c)

    def xgx(src_xl):
        return rcopy(XG.at[:, y, src_xl], XG.at[:, y, src_xl], xs_s.at[0], xs_r.at[0], near)

    def y_at(i):
        return lax.rem(y + 1 + i, Y)

    def xgy(src_y, to_y):
        return rcopy(
            XG.at[:, src_y], XG.at[:, src_y], xy_s.at[to_y], xy_r.at[src_y], (to_y * XL + xl, c)
        )

    far_p, far_m = Z // 2, Z // 2 - 1
    z_next = lax.rem(z + 1, Z)
    z_prev = lax.rem(z + Z - 1, Z)

    def behind(t):
        return lax.rem(z + Z - 1 - t, Z)

    def ahead(t):
        return lax.rem(z + 1 + t, Z)

    def a_ring(src_z, sems, to):
        block = G.at[0, xh, src_z, k]
        return rcopy(block, block, sems.at[src_z], a_r.at[src_z], z_dev(to))

    def b_ring(src_z, sems, to):
        block = G.at[1, :, src_z, k]
        return rcopy(block, block, sems.at[src_z], b_r.at[src_z], z_dev(to))

    def a_x(src_xh, src_z):
        block = G.at[0, src_xh, src_z, k]
        return rcopy(block, block, ax_s.at[src_z], ax_r.at[src_z], x_dev)

    def a_core(src_xh, src_z, src_k):
        block = G.at[0, src_xh, src_z, src_k]
        n = src_xh * Z + src_z
        return rcopy(block, block, ac_s.at[n], ac_r.at[n], core_dev)

    def b_core(src_z, src_k):
        block = G.at[1, :, src_z, src_k]
        return rcopy(block, block, bc_s.at[src_z], bc_r.at[src_z], core_dev)

    def b_x(src_xh):
        block = G.at[1, src_xh, z, k]
        return rcopy(block, block, bx_s.at[0], bx_r.at[0], x_dev)

    b_x(xh).start()
    xgx(xl).start()
    a_ring(z, ap_s, z_next).start()
    if far_m > 0:
        a_ring(z, am_s, z_prev).start()
    a_x(xh, z).start()
    a_core(xh, z, k).start()
    xgx(1 - xl).wait_recv()
    loop(Y - 1, lambda i: xgy(y, y_at(i)).start())
    b_x(1 - xh).wait_recv()
    b_ring(z, bp_s, z_next).start()
    if far_m > 0:
        b_ring(z, bm_s, z_prev).start()
    b_core(z, k).start()
    def a_step(t):
        zz = behind(t)
        a_ring(zz, ap_s, z_next).wait_recv()
        if t < far_p - 1:
            a_ring(zz, ap_s, z_next).start()
        a_x(xh, zz).start()
        a_core(xh, zz, k).start()
        if t < far_m:
            zz = ahead(t)
            a_ring(zz, am_s, z_prev).wait_recv()
            if t < far_m - 1:
                a_ring(zz, am_s, z_prev).start()
            a_x(xh, zz).start()
            a_core(xh, zz, k).start()

    def b_step(t):
        zz = behind(t)
        b_ring(zz, bp_s, z_next).wait_recv()
        if t < far_p - 1:
            b_ring(zz, bp_s, z_next).start()
        b_core(zz, k).start()
        if t < far_m:
            zz = ahead(t)
            b_ring(zz, bm_s, z_prev).wait_recv()
            if t < far_m - 1:
                b_ring(zz, bm_s, z_prev).start()
            b_core(zz, k).start()

    def cs(m):
        return rcopy(Pm.at[m, 1 - k], cr.at[m], cs_s.at[m], cs_r.at[m], core_dev)

    sel_copy.wait()
    sel2_copy.wait()

    def lower(m):
        first = sel[pl.ds(pl.multiple_of(m * (2 * s1), 16), 4 * s1), :]
        p1 = mm(first, X[:, 0:W])
        rows = sel2[pl.ds(pl.multiple_of(m * (2 * s2), 16), 4 * s2), :]
        p2 = mm(rows, X[:, W : 2 * W]) + mm(rows, X[:, 2 * W : 3 * W])
        for j in range(2):
            for core in range(CORES):
                n = 2 * j + core
                Pm[m + j, core, 0:s1, :] = p1[n * s1 : (n + 1) * s1]
                Pm[m + j, core, s1 : s1 + s2, :] = p2[n * s2 : (n + 1) * s2]
            cs(m + j).start()

    def pair_at(i):
        return 2 * lax.rem(z // 2 + 1 + i, Z // 2)

    def lower_at(n):
        lower(jnp.where(n < Z // 2, 1 - xh, xh) * Z + pair_at(lax.rem(n, Z // 2)))

    a_step(0)
    for t in range(1, far_p):
        a_step(t)
        b_step(t - 1)
    loop(Y - 1, lambda i: xgy(y_at(i), y).wait_recv())
    x1t = XG[0].reshape(W, ncol)
    lct = XG[1].reshape(W, ncol)
    clt = cl_ref[...].astype(F32).T.astype(BF16)
    x2 = (lct.astype(F32) - mm(clt, x1t)).T
    x2hi = x2.astype(BF16)
    X[:, 0:W] = x1t.astype(F32).T.astype(BF16)
    X[:, W : 2 * W] = x2hi
    X[:, 2 * W : 3 * W] = (x2 - x2hi.astype(F32)).astype(BF16)

    loop(Z // 2, lower_at)

    def over(i):
        zz = z_at(i)
        a_x(1 - xh, zz).wait_recv()
        a_core(1 - xh, zz, k).start()

    loop(Z, over)
    def rx(zz):
        return rcopy(xs.at[zz], xr.at[zz], rx_s.at[zz], rx_r.at[zz], x_dev)

    def rz(src_z, to_z):
        return rcopy(zs.at[to_z], zr.at[src_z], rz_s.at[to_z], rz_r.at[src_z], z_dev(to_z))

    def to_x(i):
        zz = z_at(i)
        m = (1 - xh) * Z + zz
        cs(m).wait_recv()
        xs[zz] = (Pm[m, k] + cr[m]).astype(BF16)
        rx(zz).start()

    loop(Z, to_x)

    loop(Z // 2, lambda i: lower_at(Z // 2 + i))


    def pu(j, src_r, to_r):
        return rcopy(
            PUb.at[j, to_r],
            ur_buf.at[j, src_r],
            pu_s.at[j, to_r],
            pu_r.at[j, src_r],
            row_dev(to_r),
        )

    loop(M, lambda i: a_core(i // Z, lax.rem(i, Z), 1 - k).wait_recv())
    PU[0] = mm(G[0].reshape(W, nb1 * B), sel[...])
    PUb[0] = PU[0].astype(BF16).reshape(R, uw, ncol)
    loop(R - 1, lambda i: pu(0, r, r_at(i)).start())

    b_step(far_p - 1)
    loop(Z, lambda i: b_core(i, 1 - k).wait_recv())
    cu = cu_ref[...]
    wide = 2 * B if nb1 % 2 == 0 else B

    def second(j):
        at = pl.ds(pl.multiple_of(j * wide, wide), wide)
        up = G[0, :, :, :, :, at].reshape(W, wide)
        uc = G[1, :, :, :, :, at].reshape(W, wide)
        v = uc.astype(F32) - mm(cu, up)
        hi = v.astype(BF16)
        V[0, :, at] = hi
        V[1, :, at] = (v - hi.astype(F32)).astype(BF16)

    loop(nb1 * B // wide, second)

    def both(j):
        PU[1 + j] = mm(V[j], sel[...])

    loop(2, both)
    PU[1] = PU[1] + PU[2]
    PUb[1] = PU[1].astype(BF16).reshape(R, uw, ncol)
    loop(R - 1, lambda i: pu(1, r, r_at(i)).start())

    def to_z(i):
        zz = z_at(i)
        m = xh * Z + zz
        cs(m).wait_recv()
        rx(zz).wait_recv()
        total = Pm[m, k] + cr[m] + xr[zz].astype(F32)

        @pl.when(i < Z - 1)
        def _():
            zs[zz] = total.astype(BF16)
            rz(z, zz).start()

        @pl.when(i == Z - 1)
        def _():
            own[...] = total

    loop(Z, to_z)


    tail[...] = dg2_ref[...] + exact(
        cu.astype(F32), exact(dg1_ref[...], cl_ref[...].astype(F32))
    )

    mine = pl.ds(pl.multiple_of(r * uw, 16), uw)

    def from_r(i):
        rr = r_at(i)
        for j in range(2):
            pu(j, rr, r).wait_recv()
            PU[j, mine, :] = PU[j, mine, :] + ur_buf[j, rr].astype(F32)

    loop(R - 1, from_r)
    u1 = (-PU[0, mine, :]).astype(BF16)
    u2 = (-PU[1, mine, :]).astype(BF16)
    dd[0] = mm(u1, X[:, 0:W])
    dd[1] = mm(u2, X[:, W : 2 * W]) + mm(u2, X[:, 2 * W : 3 * W])
    me = xh * CORES + k

    def d_four(src, half, to_, dev):
        return rcopy(dd.at[half], drc.at[src], d_s.at[to_], d_r.at[src], dev)

    core_at, x_at, cross_at = xh * CORES + 1 - k, (1 - xh) * CORES + k, (1 - xh) * CORES + 1 - k
    sends = (
        d_four(me, 1 - k, core_at, core_dev),
        d_four(me, k, x_at, x_dev),
        d_four(me, 1 - k, cross_at, cross_dev),
    )
    for send in sends:
        send.start()
    drc[me] = dd[k]
    u1_out[...] = u1
    u2_out[...] = mm(u2, pick_cols[...]).astype(BF16)

    for src in (core_at, x_at, cross_at):
        d_four(src, k, me, x_dev).wait_recv()
    dz[z] = ((drc[0] + drc[1]) + (drc[2] + drc[3])).astype(BF16)

    def dzc(src_z, to_z):
        return rcopy(dz.at[src_z], dz.at[src_z], dz_s.at[to_z], dz_r.at[src_z], z_dev(to_z))

    loop(Z - 1, lambda i: dzc(z, z_at(i)).start())
    loop(Z - 1, lambda i: dzc(z_at(i), z).wait_recv())
    total = dz[0].astype(F32)
    for i in range(1, Z):
        total = total + dz[i].astype(F32)
    Dall[k, r] = total

    def drow(src_r, to_r):
        return rcopy(
            Dall.at[k, src_r], Dall.at[k, src_r], dr_s.at[to_r], dr_r.at[src_r], row_dev(to_r)
        )

    def d_core(src_r, src_k):
        block = Dall.at[src_k, src_r]
        return rcopy(block, block, df_s.at[src_r], df_r.at[src_r], core_dev)

    loop(R - 1, lambda i: drow(r, r_at(i)).start())
    d_core(r, k).start()
    def from_z(i):
        zz = z_at(i)
        rz(zz, z).wait_recv()
        own[...] = own[...] + zr[zz].astype(F32)

    loop(Z - 1, from_z)
    l1_out[...] = (-own[0:s1, :]).astype(BF16)
    l2_out[...] = (-own[s1 : s1 + s2, :]).astype(BF16)


    def from_row(i):
        rr = r_at(i)
        drow(rr, r).wait_recv()
        d_core(rr, k).start()

    loop(R - 1, from_row)
    loop(R, lambda i: d_core(i, 1 - k).wait_recv())
    d1_out[...] = dg1_ref[...] - Dall[0].reshape(W, W)
    d2_out[...] = tail[...] - Dall[1].reshape(W, W)

    def left_z(i):
        zz = z_at(i)
        rz(z, zz).wait_send()
        dzc(z, zz).wait_send()

    def left_r(i):
        rr = r_at(i)
        pu(0, r, rr).wait_send()
        pu(1, r, rr).wait_send()
        drow(r, rr).wait_send()

    def left_x(i):
        a_x(xh, i).wait_send()
        rx(i).wait_send()
        b_core(i, k).wait_send()

    def left_c(i):
        a_core(i // Z, lax.rem(i, Z), k).wait_send()
        cs(i).wait_send()

    b_x(xh).wait_send()
    xgx(xl).wait_send()
    loop(Y - 1, lambda i: xgy(y, y_at(i)).wait_send())
    for t in range(far_p):
        a_ring(lax.rem(z + Z - t, Z), ap_s, z_next).wait_send()
        b_ring(lax.rem(z + Z - t, Z), bp_s, z_next).wait_send()
    for t in range(far_m):
        a_ring(lax.rem(z + t, Z), am_s, z_prev).wait_send()
        b_ring(lax.rem(z + t, Z), bm_s, z_prev).wait_send()
    loop(Z - 1, left_z)
    loop(R - 1, left_r)
    loop(Z, left_x)
    loop(M, left_c)
    loop(R, lambda i: d_core(i, k).wait_send())
    for send in sends:
        send.wait_send()


def pick(
    R,
    C,
    one_ref,
    two_ref,
    sep,
    lp_ref,
    lc_ref,
    up_ref,
    uc_ref,
    sel,
    sel2,
    own_u,
    own_x,
    pick_cols,
):
    r = lax.axis_index("row")
    c = lax.axis_index("col")
    runs = C // R
    nb1 = runs * ONE
    ur = up_ref.shape[0]
    lw = lp_ref.shape[0]

    def one_at(run, s):
        return one_ref[run * ONE + s]

    def two_at(run, t):
        return two_ref[run * TWO + t]

    def in_two(run, b):
        hit = (two_at(run, 0) == b).astype(jnp.int32)
        for t in range(1, TWO):
            hit = hit + (two_at(run, t) == b).astype(jnp.int32)
        return hit

    col_at = [pl.multiple_of((one_at(c, s) - c * SPAN) * B, B) for s in range(ONE)]

    def row_at(b):
        return pl.multiple_of((b - r * (runs * SPAN)) * B, B)

    def some_run(q, carry):
        run = r * runs + q
        for s in range(ONE):
            b = one_at(run, s)
            at = row_at(b)
            to = pl.ds(pl.multiple_of((q * ONE + s) * B, B), B)
            for t in range(ONE):
                sel[to, t * B : (t + 1) * B] = sep[pl.ds(at, B), pl.ds(col_at[t], B)]
            own_u[0, :, to] = up_ref[:, pl.ds(at, B)]
            piece = uc_ref[:, pl.ds(at, B)].astype(F32)
            hit = jnp.full((ur, B), in_two(run, b))
            own_u[1, :, to] = jnp.where(hit > 0, piece, 0.0).astype(BF16)
        for t in range(TWO):
            at = row_at(two_at(run, t))
            to = pl.ds(pl.multiple_of((q * TWO + t) * B, B), B)
            for s in range(ONE):
                sel2[to, s * B : (s + 1) * B] = sep[pl.ds(at, B), pl.ds(col_at[s], B)]
        return carry

    lax.fori_loop(0, runs, some_run, 0)

    same = lax.broadcasted_iota(jnp.int32, (B, B), 0) == lax.broadcasted_iota(jnp.int32, (B, B), 1)
    eye = jnp.where(same, 1.0, 0.0)
    for s in range(ONE):
        b = one_at(c, s)
        to = pl.ds(s * B, B)
        own_x[0, :, to] = lp_ref[:, pl.ds(col_at[s], B)]
        piece = lc_ref[:, pl.ds(col_at[s], B)].astype(F32)
        hit = jnp.full((lw, B), in_two(c, b))
        own_x[1, :, to] = jnp.where(hit > 0, piece, 0.0).astype(BF16)
        for t in range(TWO):
            hit = jnp.full((B, B), (two_at(c, t) == b).astype(jnp.int32))
            pick_cols[to, t * B : (t + 1) * B] = jnp.where(hit > 0, eye, 0.0).astype(BF16)


def hand_over(*refs):
    n = (len(refs) - 1) // 2
    copies = [pltpu.make_async_copy(refs[i], refs[n + i], refs[-1].at[i]) for i in range(n)]
    for copy in copies:
        copy.start()
    for copy in copies:
        copy.wait()


def on_device(
    R,
    C,
    inv_sep,
    lower_one,
    upper_one,
    diag_inv_one,
    blocks_one,
    lower_two,
    upper_two,
    corner_lower,
    corner_upper,
    diag_inv_two,
    blocks_two,
):
    W = diag_inv_one.shape[0]
    Z = C // (XH * CORES)
    M = XH * Z
    runs = C // R
    nb1 = runs * ONE
    ncol = ONE * B
    ur, lw, uw = W // C, W // R, W // R
    s1, s2 = ONE * B // R, TWO * B // R
    sh = s1 + s2
    vmem = pl.BlockSpec(memory_space=pltpu.VMEM)
    hbm = pl.BlockSpec(memory_space=pltpu.HBM)
    smem = pl.BlockSpec(memory_space=pltpu.SMEM)
    dma = pltpu.SemaphoreType.DMA
    picked = pl.pallas_call(
        functools.partial(pick, R, C),
        out_shape=(
            jax.ShapeDtypeStruct((nb1 * B, ncol), BF16),
            jax.ShapeDtypeStruct((runs * TWO * B, ncol), BF16),
            jax.ShapeDtypeStruct((2, ur, nb1 * B), BF16),
            jax.ShapeDtypeStruct((2, lw, ncol), BF16),
            jax.ShapeDtypeStruct((ncol, TWO * B), BF16),
        ),
        in_specs=[smem, smem] + [vmem] * 5,
        out_specs=(vmem,) * 5,
        compiler_params=pltpu.CompilerParams(vmem_limit_bytes=24 * 2**20),
        name="pick",
    )(blocks_one, blocks_two, inv_sep, lower_one.T, lower_two.T, upper_one, upper_two)
    results = pl.pallas_call(
        functools.partial(kernel, R, C, W),
        out_shape=(
            jax.ShapeDtypeStruct((s1, W), BF16),
            jax.ShapeDtypeStruct((uw, ncol), BF16),
            jax.ShapeDtypeStruct((W, W), F32),
            jax.ShapeDtypeStruct((s2, W), BF16),
            jax.ShapeDtypeStruct((uw, TWO * B), BF16),
            jax.ShapeDtypeStruct((W, W), F32),
        ),
        in_specs=[pl.BlockSpec(memory_space=pl.ANY)] * 2 + [vmem] * 7,
        out_specs=(vmem,) * 6,
        scratch_shapes=[
            pltpu.VMEM((nb1 * B, ncol), BF16),
            pltpu.VMEM((runs * TWO * B, ncol), BF16),
            pltpu.VMEM((2, XH, Z, CORES, ur, nb1 * B), BF16),
            pltpu.VMEM((2, W, nb1 * B), BF16),
            pltpu.VMEM((2, R // XL, XL, lw, ncol), BF16),
            pltpu.VMEM((ncol, 3 * W), BF16),
            pltpu.VMEM((M, 2, sh, W), F32),
            pltpu.VMEM((M, sh, W), F32),
            pltpu.VMEM((Z, sh, W), BF16),
            pltpu.VMEM((Z, sh, W), BF16),
            pltpu.VMEM((Z, sh, W), BF16),
            pltpu.VMEM((Z, sh, W), BF16),
            pltpu.VMEM((sh, W), F32),
            pltpu.VMEM((3, W, ncol), F32),
            pltpu.VMEM((2, R, uw, ncol), BF16),
            pltpu.VMEM((2, R, uw, ncol), BF16),
            pltpu.VMEM((2, uw, W), F32),
            pltpu.VMEM((XH * CORES, uw, W), F32),
            pltpu.VMEM((Z, uw, W), BF16),
            pltpu.VMEM((2, R, uw, W), F32),
            pltpu.VMEM((W, W), F32),
        ]
        + [dma((n,)) for n in (2, 1, 1, R // XL, R // XL)]
        + [dma((n,)) for n in (Z, Z, Z, Z, Z, Z, Z, Z, M, M, Z, Z, 1, 1)]
        + [dma((n,)) for n in (M, M, Z, Z, Z, Z)]
        + [dma((2, R)), dma((2, R))]
        + [dma((n,)) for n in (4, 4, Z, Z, R, R, R, R)],
        compiler_params=pltpu.CompilerParams(
            collective_id=0, has_side_effects=True, vmem_limit_bytes=40 * 2**20
        ),
        name="panels",
    )(*picked, corner_lower, corner_upper, diag_inv_one, diag_inv_two)
    return pl.pallas_call(
        hand_over,
        out_shape=tuple(jax.ShapeDtypeStruct(a.shape, a.dtype) for a in results),
        in_specs=[vmem] * len(results),
        out_specs=(hbm,) * len(results),
        scratch_shapes=[dma((len(results),))],
        compiler_params=pltpu.CompilerParams(vmem_limit_bytes=4 * 2**20),
        name="hand_over",
    )(*results)


def solution(mesh):
    R, C = mesh.shape["row"], mesh.shape["col"]
    return jax.shard_map(
        functools.partial(on_device, R, C),
        mesh=mesh,
        in_specs=(
            P("row", "col"),
            P("col", "row"),
            P("col", "row"),
            P(),
            P(),
            P("col", "row"),
            P("col", "row"),
            P(),
            P(),
            P(),
            P(),
        ),
        out_specs=(
            P(("row", "col"), None),
            P("row", "col"),
            P(),
            P(("row", "col"), None),
            P("row", "col"),
            P(),
        ),
        check_vma=False,
    )
```
